512 devices in a mesh: ctx: 64 (over y_hi, x, z), dp: 8 (over y_lo, core).
Axes of the slice: x: 4, y: 8 (y_hi: 2, y_lo: 4; y = y_hi * 4 + y_lo), z: 8, core: 2. Of those that a mesh axis runs over, the one named last changes fastest.
Arguments:
- queries: bfloat16 [8192, 2048], P('ctx', 'dp'), may hold values from -192 to 192
- keys: bfloat16 [8192, 128], P('ctx'), may hold values from -32 to 32
- values: bfloat16 [8192, 128], P('ctx'), may hold values from -6 to 6
- out_grads: bfloat16 [8192, 2048], P('ctx', 'dp'), may hold values from -6 to 6
- doc_lengths: int32 [32], replicated, may hold values from 1 to 4224, 8192 in all
Outputs:
- query_grads: bfloat16 [8192, 2048], P('ctx', 'dp')
- key_grads: bfloat16 [8192, 128], P(('ctx', 'dp'))
- value_grads: bfloat16 [8192, 128], P(('ctx', 'dp'))
The draws below stay inside these ranges and needn't reach their ends.
Inputs may be any that keep to these rules, and one draw needn't show every extreme that they name: `doc_lengths`: document lengths in order of position; they sum to 8192 and the longest document has exactly 4224 tokens.
All inputs are finite; a program needn't handle non-finite values.
Results may differ from the reference program's by a relative error of at most 0.023.
Values may be sent and summed in bfloat16 or wider, within the bound.
A program may use at most 64 MiB of HBM per device.

```python
import math
import jax
import jax.numpy as jnp
import numpy as np
from jax import lax

HD = 128
GROUP = 16
TOK_DEV = 128
SPAN = 64
NCHUNK = 128
SEQ = 8192
MAXDOC = 4224
NDOCS = 32


def key_table(key):
    noise_rows = jnp.clip(jax.random.normal(jax.random.fold_in(key, 101), (SEQ, HD), jnp.float32), -6.0, 6.0)
    return noise_rows


def draw_keys(key, part):
    return key_table(key).astype(jnp.bfloat16)


def draw_queries(key, part):
    base_rows = jnp.clip(jax.random.normal(jax.random.fold_in(key, 201), (SEQ, GROUP, HD), jnp.float32), -6.0, 6.0)
    return base_rows.reshape(SEQ, GROUP * HD).astype(jnp.bfloat16)


def steps_of(stream_key, extent, shards, low, top_value):
    def one(dim, parts):
        steps = jax.random.uniform(jax.random.fold_in(jax.random.fold_in(stream_key, 6), dim), (parts,), jnp.float32, low / len(shards), top_value / len(shards))
        return jnp.repeat(jnp.exp(steps), extent[dim] // parts).reshape((-1,) + (1,) * (len(extent) - dim - 1))

    factor_of = one(*shards[0])
    for cut in shards[1:]:
        factor_of = factor_of * one(*cut)
    return factor_of


def profile(number_of, total, limit, lean):
    loads = [(1 << 20) // math.isqrt(rank ** lean) + 1 for rank in range(2, number_of + 1)]
    rest, holding = total - limit - (number_of - 1), [1] * (number_of - 1)
    while rest > 0:
        free = [i for i in range(number_of - 1) if holding[i] < limit]
        pool, remaining = sum([loads[i] for i in free]), rest
        for i in free:
            extra = min(limit - holding[i], max(1, remaining * loads[i] // pool), rest)
            holding[i] = holding[i] + extra
            rest = rest - extra
    return np.array([limit] + holding)


def ragged_sizes(stream_key, count, total, bound, slope):
    if count == 2:
        one = jax.random.randint(stream_key, (), max(1, total - bound), min(bound, total - 1) + 1)
        return jnp.stack([one, total - one])
    lengths = jnp.asarray(profile(count, total, bound, slope), jnp.int32)
    pairs = (count - 1) // 2
    source_of, taker = lengths[1:1 + 2 * pairs:2], lengths[2:2 + 2 * pairs:2]
    margin = jnp.minimum(source_of - 1, bound - taker)
    shifted = jax.random.randint(jax.random.fold_in(stream_key, 1), (pairs,), 0, 1 << 20) % (margin + 1)
    lengths = lengths.at[1:1 + 2 * pairs:2].set(source_of - shifted).at[2:2 + 2 * pairs:2].set(taker + shifted)
    return lengths[jax.random.permutation(jax.random.fold_in(stream_key, 2), count)]


def gaussian(key, extent, deviation, limit, cuts=(), held_as=jnp.bfloat16):
    entries = deviation * jax.random.normal(key, extent, jnp.float32)
    if cuts:
        entries = entries * steps_of(key, extent, cuts, -0.22, 0.18)
    return jnp.clip(entries, -limit, limit).astype(held_as)


def setup_inputs(seed: int = 0) -> dict:
    arg_keys = jax.random.split(jax.random.key(seed), 6)
    queries = draw_queries(jax.random.fold_in(arg_keys[5], 71), 0)
    keys = draw_keys(jax.random.fold_in(arg_keys[5], 71), 0)
    values = gaussian(arg_keys[2], (SEQ, HD), 1.0, 6.0, ((0, 64),))
    out_grads = gaussian(arg_keys[3], (SEQ, GROUP * HD), 1.0, 6.0, ((0, 64), (1, 8)))
    doc_lengths = ragged_sizes(arg_keys[4], NDOCS, SEQ, MAXDOC, 1).astype(jnp.int32)
    return dict(queries=queries, keys=keys, values=values, out_grads=out_grads, doc_lengths=doc_lengths)


masked_value = -1.0e30


def token_positions():
    row_ids = jnp.arange(SEQ, dtype=jnp.int32)
    device_ids = row_ids // TOK_DEV
    offsets = row_ids % TOK_DEV
    low_pos = device_ids * SPAN + offsets
    high_pos = (NCHUNK - 1 - device_ids) * SPAN + offsets - SPAN
    return jnp.where(offsets < SPAN, low_pos, high_pos)


def reference(queries, keys, values, out_grads, doc_lengths):
    positions = token_positions()
    doc_ends = jnp.cumsum(doc_lengths)
    doc_index = jnp.sum((positions[:, None] >= doc_ends[None, :]).astype(jnp.int32), axis=1)
    live_mask = (positions[None, :] <= positions[:, None]) & (doc_index[None, :] == doc_index[:, None])
    score_scale = HD ** -0.5

    def one_head(head_id):
        start = (head_id * HD).astype(jnp.int32)
        query_head = lax.dynamic_slice_in_dim(queries, start, HD, 1)
        grad_head = lax.dynamic_slice_in_dim(out_grads, start, HD, 1)
        logits = score_scale * jnp.dot(query_head, keys.T, preferred_element_type=jnp.float32)
        row_top = jnp.max(jnp.where(live_mask, logits, masked_value), axis=1, keepdims=True)
        row_total = jnp.sum(jnp.where(live_mask, jnp.exp(logits - row_top), 0.0), axis=1, keepdims=True)
        row_lse = row_top + jnp.log(row_total)
        weights_f = jnp.where(live_mask, jnp.exp(logits - row_lse), 0.0)
        weights_low = weights_f.astype(jnp.bfloat16)
        output = jnp.dot(weights_low, values, preferred_element_type=jnp.float32)
        delta = jnp.sum(grad_head.astype(jnp.float32) * output, axis=1, keepdims=True)
        dweights = jnp.dot(grad_head, values.T, preferred_element_type=jnp.float32)
        dlogits = (weights_f * (dweights - delta)).astype(jnp.bfloat16)
        query_grad = (score_scale * jnp.dot(dlogits, keys, preferred_element_type=jnp.float32)).astype(jnp.bfloat16)
        key_part = jnp.dot(dlogits.T, query_head, preferred_element_type=jnp.float32)
        value_part = jnp.dot(weights_low.T, grad_head, preferred_element_type=jnp.float32)
        return query_grad, key_part, value_part

    query_parts, key_parts, value_parts = lax.map(one_head, jnp.arange(GROUP, dtype=jnp.int32))
    query_grads = jnp.transpose(query_parts, (1, 0, 2)).reshape(SEQ, GROUP * HD)
    key_grads = (score_scale * jnp.sum(key_parts, axis=0)).astype(jnp.bfloat16)
    value_grads = jnp.sum(value_parts, axis=0).astype(jnp.bfloat16)
    return (query_grads, key_grads, value_grads)
```

```python
import jax
import jax.numpy as jnp
from jax import lax
from jax.experimental import pallas as pl
from jax.experimental.pallas import tpu as pltpu
from jax.sharding import PartitionSpec as P

MESH = pl.DeviceIdType.MESH
NH, NX, NZ, NY = 2, 4, 8, 4
NDP = 2 * NY
HD, SPAN, NDOCS = 128, 64, 32
BLOCK = 16
PAIR = 2 * SPAN
GROUPS = 2
PER = NDP // GROUPS
ROWS = PER * PAIR
TILE = 256
LAST = 127
REACH = 66
LOW, FLOOR = -1e30, -1e29
SCALE = HD**-0.5
LOG2E = 1.4426950408889634
F32, BF16 = jnp.float32, jnp.bfloat16


def dot(a, b, dims):
    return lax.dot_general(a, b, (dims, ((), ())), preferred_element_type=F32)


def kernel(
    q_hbm, k_hbm, v_hbm, g_hbm, lens_hbm,
    dq_out, dk_out, dv_out,
    qg, kv, acc, dqa, qpos, qbeg, run, stat, stat_r, fin, lse, delta,
    dq_sib, dq_sib_r, dq_own, dq_s, dq_r, x_s, x_r, own_x, z_s, z_r,
    lens, loc, send, recv,
):
    ctx, dp = lax.axis_index("ctx"), lax.axis_index("dp")
    h, x, z = lax.div(ctx, 32), lax.rem(lax.div(ctx, 8), 4), lax.rem(ctx, 8)
    y, c = lax.div(dp, 2), lax.rem(dp, 2)
    t, s = lax.div(y, 2), lax.rem(y, 2)
    odd, zh = lax.rem(z, 2), lax.div(z, 2)
    in_span = BLOCK * (2 * s + c)
    block = 4 * lax.rem(t + z, 2) + 2 * s + c
    across = 4 * (1 - t) + 2 * s + c

    def at(dh, dz):
        return lax.rem(h + dh, NH) * 32 + x * 8 + lax.rem(z + dz, NZ)

    ys = [(ctx, 2 * lax.rem(y + d, NY) + c) for d in range(1, NY)]
    dps = [(ctx, lax.rem(dp + d, NDP)) for d in range(1, NDP)]
    offsets = [(1, dz) for dz in range(NZ)] + [(0, dz) for dz in range(1, NZ)]
    hzs = [at(dh, dz) for dh, dz in offsets]
    xs = [(h * 32 + lax.rem(x + d, NX) * 8 + z, dp) for d in range(1, NX)]
    sibling = (ctx, 2 * y + 1 - c)

    sent = []

    def remote(src, dst, n, to):
        return pltpu.make_async_remote_copy(
            src_ref=src, dst_ref=dst, send_sem=send.at[n], recv_sem=recv.at[n],
            device_id=to, device_id_type=MESH,
        )

    def go(copy):
        copy.start()
        sent.append(copy)
        return copy

    rows = pl.ds(pl.multiple_of(block * BLOCK, BLOCK), BLOCK)
    mine = kv.at[h, x, odd, zh]
    local_kv = [
        pltpu.make_async_copy(k_hbm.at[rows, :], mine.at[:, 0:HD], loc.at[0]),
        pltpu.make_async_copy(v_hbm.at[rows, :], mine.at[:, HD : 2 * HD], loc.at[1]),
    ]
    local_qg = [
        pltpu.make_async_copy(
            ref.at[span * SPAN : (span + 1) * SPAN, head * HD : (head + 1) * HD],
            qg.at[dp, kind, span, head * SPAN : (head + 1) * SPAN, :],
            loc.at[2 + 4 * kind + 2 * span + head],
        )
        for kind, ref in enumerate((q_hbm, g_hbm))
        for span in range(2)
        for head in range(2)
    ]
    local_lens = pltpu.make_async_copy(lens_hbm, lens, loc.at[10])

    barrier = pltpu.get_barrier_semaphore()
    partners = [(to, dp) for to in hzs] + xs + dps
    for to in partners:
        pl.semaphore_signal(barrier, inc=1, device_id=to, device_id_type=MESH)

    @pl.when(odd == 1)
    def _():
        for to in hzs:
            pl.semaphore_signal(barrier, inc=1, device_id=(to, across), device_id_type=MESH)

    for copy in local_kv + local_qg + [local_lens]:
        copy.start()
    pl.semaphore_wait(barrier, len(partners) + 8 - odd)

    for copy in local_kv:
        copy.wait()
    to_hz = [go(remote(mine, mine, n, (to, dp))) for n, to in enumerate(hzs)]
    for copy in local_qg:
        copy.wait()
    own = qg.at[dp]
    to_y = [go(remote(own, own, 14 + d, ys[d - 1])) for d in range(1, NY)]
    to_sib = [go(remote(own, own, 18, sibling))]
    for copy in to_hz:
        copy.wait_recv()
    plane = kv.at[:, x]
    to_x = [go(remote(plane, plane, 18 + d, xs[d - 1])) for d in range(1, NX)]

    local_lens.wait()
    token = lax.rem(lax.broadcasted_iota(jnp.int32, (1, ROWS), 1), SPAN)
    for span, first in ((0, ctx * SPAN), (1, (LAST - ctx) * SPAN)):
        pos = first + token
        begin = jnp.zeros_like(pos)
        end = jnp.int32(0)
        for n in range(NDOCS):
            end = end + lens[n]
            begin = jnp.where(pos >= end, end, begin)
        qpos[span] = pos
        qbeg[span] = begin

    acc[...] = jnp.zeros_like(acc)
    dqa[...] = jnp.zeros_like(dqa)
    stat[...] = jnp.zeros_like(stat)
    run[0] = jnp.full(run.shape[1:], FLOOR, F32)
    run[1] = jnp.zeros(run.shape[1:], F32)
    run[2] = jnp.zeros(run.shape[1:], F32)
    for d in range(1, NY):
        to_y[d - 1].wait_recv()
        got = qg.at[2 * lax.rem(y + NY - d, NY) + c]
        to_sib.append(go(remote(got, got, 21 + d, sibling)))
    for copy in to_x + to_sib:
        copy.wait_recv()

    n_a = lax.div(ctx, 32) + 1
    from_b = lax.div(jnp.maximum(LAST - REACH - ctx, 0), 32)
    n_b = NH - from_b
    from_c = lax.div(ctx, 32)
    n_tiles = GROUPS * (n_a + n_b + NH - from_c)
    row = lax.broadcasted_iota(jnp.int32, (TILE, 1), 0)
    row_ctx = 8 * lax.div(row, 64) + 2 * lax.rem(lax.div(row, BLOCK), 4)
    row_in = in_span + lax.rem(row, BLOCK)

    def tile(i):
        n, group = lax.div(i, GROUPS), lax.rem(i, GROUPS)
        span = jnp.where(n < n_a, 0, 1)
        half = jnp.where(n < n_a + n_b, 0, 1)
        hi = jnp.where(n < n_a, n, jnp.where(n < n_a + n_b, from_b + n - n_a, from_c + n - n_a - n_b))
        zp = lax.rem(t + half, 2)
        k = kv[hi, :, zp, :, :, 0:HD].reshape(TILE, HD)
        v = kv[hi, :, zp, :, :, HD : 2 * HD].reshape(TILE, HD)
        q = qg[pl.ds(PER * group, PER), 0, span].reshape(ROWS, HD)
        g = qg[pl.ds(PER * group, PER), 1, span].reshape(ROWS, HD)
        of = hi * 32 + zp + row_ctx
        kpos = jnp.where(half == 0, of, LAST - of) * SPAN + row_in
        live = (kpos <= qpos[span]) & (kpos >= qbeg[span])
        logits = dot(k, q, ((1,), (1,))) * (SCALE * LOG2E)
        dweights = dot(v, g, ((1,), (1,)))
        return span, group, hi, zp, k, q, g, live, logits, dweights

    def forward(i, _):
        span, group, hi, zp, k, q, g, live, logits, dweights = tile(i)
        logits = jnp.where(live, logits, LOW)
        old = run[0, span, group]
        top = jnp.maximum(old, jnp.max(logits, axis=0, keepdims=True))
        terms = jnp.exp2(logits - top)
        keep = jnp.exp2(old - top)
        run[0, span, group] = top
        run[1, span, group] = run[1, span, group] * keep + jnp.sum(terms, axis=0, keepdims=True)
        run[2, span, group] = run[2, span, group] * keep + jnp.sum(terms * dweights, axis=0, keepdims=True)
        return 0

    lax.fori_loop(0, n_tiles, forward, 0)

    for j in range(NDP):
        lanes = pl.ds((j % PER) * PAIR, PAIR)
        for kind in range(3):
            for span in range(2):
                n = 2 * kind + span
                stat[j, n : n + 1] = run[kind, span, j // PER, :, lanes]
    to_stat = [
        go(remote(stat.at[dps[d - 1][1]], stat_r.at[d], 24 + d, dps[d - 1])) for d in range(1, NDP)
    ]
    stat_r[0] = stat[dp]
    for copy in to_stat:
        copy.wait_recv()
    top = stat_r[0, 0:2]
    for d in range(1, NDP):
        top = jnp.maximum(top, stat_r[d, 0:2])
    total, moment = jnp.zeros_like(top), jnp.zeros_like(top)
    for d in range(NDP):
        part = jnp.exp2(stat_r[d, 0:2] - top)
        total = total + part * stat_r[d, 2:4]
        moment = moment + part * stat_r[d, 4:6]
    fin[dp, 0:2] = top + jnp.log(total) * LOG2E
    fin[dp, 2:4] = moment / total
    fin[dp, 4:8] = jnp.zeros((4, PAIR), F32)
    to_fin = [go(remote(fin.at[dp], fin.at[dp], 31 + d, dps[d - 1])) for d in range(1, NDP)]
    for copy in to_fin:
        copy.wait_recv()
    for j in range(NDP):
        lanes = pl.ds((j % PER) * PAIR, PAIR)
        for span in range(2):
            lse[span, j // PER, :, lanes] = fin[j, span : span + 1]
            delta[span, j // PER, :, lanes] = fin[j, 2 + span : 3 + span]

    def backward(i, _):
        span, group, hi, zp, k, q, g, live, logits, dweights = tile(i)
        weights = jnp.where(live, jnp.exp2(logits - lse[span, group]), 0.0)
        dlogits = (weights * (dweights - delta[span, group])).astype(BF16)
        acc[hi, :, zp, :, :, 0:HD] += dot(dlogits, q, ((1,), (0,))).reshape(NX, 4, BLOCK, HD)
        acc[hi, :, zp, :, :, HD : 2 * HD] += dot(weights.astype(BF16), g, ((1,), (0,))).reshape(NX, 4, BLOCK, HD)
        dqa[pl.ds(PER * group, PER), span] += dot(dlogits, k, ((0,), (0,))).reshape(PER, PAIR, HD)
        return 0

    lax.fori_loop(0, n_tiles, backward, 0)

    to_rx = []
    for d in range(1, NX):
        x_s[d - 1] = acc[:, lax.rem(x + d, NX)].astype(BF16)
        to_rx.append(go(remote(x_s.at[d - 1], x_r.at[d - 1], 38 + d, xs[d - 1])))
    to_ds = []
    for n in range(NY):
        of = lax.rem(y + 1 + n, NY)
        dq_sib[n] = dqa[2 * of + 1 - c].astype(BF16)
        to_ds.append(go(remote(dq_sib.at[n], dq_sib_r.at[n], 42 + n, sibling)))
    to_dq = []
    for n in range(NY):
        of = lax.rem(y + 1 + n, NY)
        to_ds[n].wait_recv()
        both = dqa[2 * of + c] + dq_sib_r[n].astype(F32)
        if n < NY - 1:
            dq_s[n] = both.astype(BF16)
            to_dq.append(go(remote(dq_s.at[n], dq_r.at[n], 46 + n, ys[n])))
        else:
            dq_own[...] = both

    for copy in to_rx:
        copy.wait_recv()
    own_x[...] = acc[:, x] + x_r[0].astype(F32) + x_r[1].astype(F32) + x_r[2].astype(F32)
    to_rz = []
    for n, (dh, dz) in enumerate(offsets):
        zz = lax.rem(z + dz, NZ)
        z_s[n] = own_x[lax.rem(h + dh, NH), lax.rem(zz, 2), lax.div(zz, 2)].astype(BF16)
        to_rz.append(
            go(remote(z_s.at[n], z_r.at[n], 49 + n, (hzs[n], jnp.where(lax.rem(zz, 2) == 1, across, dp))))
        )
    z_s[15] = own_x[h, odd, zh].astype(BF16)
    near = remote(z_s.at[15], z_r.at[15], 64, (ctx, across))

    @pl.when(odd == 1)
    def _():
        near.start()

    @pl.when(odd == 0)
    def _():
        z_r[15] = z_s[15]

    for copy in to_dq:
        copy.wait_recv()
    total_dq = (SCALE * (dq_own[...] + dq_r[0].astype(F32) + dq_r[1].astype(F32) + dq_r[2].astype(F32))).astype(BF16)
    for span in range(2):
        for head in range(2):
            dq_out[span * SPAN : (span + 1) * SPAN, head * HD : (head + 1) * HD] = total_dq[
                span, head * SPAN : (head + 1) * SPAN
            ]

    for copy in to_rz:
        copy.wait_recv()

    @pl.when(odd == 1)
    def _():
        near.wait_recv()
        near.wait_send()

    total_kv = z_r[0].astype(F32)
    for n in range(1, 16):
        total_kv = total_kv + z_r[n].astype(F32)
    dk_out[...] = (SCALE * total_kv[:, 0:HD]).astype(BF16)
    dv_out[...] = total_kv[:, HD : 2 * HD].astype(BF16)

    for copy in sent:
        copy.wait_send()


def body(queries, keys, values, out_grads, doc_lengths):
    vmem, hbm = pltpu.VMEM, pl.BlockSpec(memory_space=pltpu.HBM)
    whole = pl.BlockSpec(memory_space=pltpu.VMEM)
    return pl.pallas_call(
        kernel,
        out_shape=(
            jax.ShapeDtypeStruct(queries.shape, BF16),
            jax.ShapeDtypeStruct((BLOCK, HD), BF16),
            jax.ShapeDtypeStruct((BLOCK, HD), BF16),
        ),
        in_specs=[hbm] * 5,
        out_specs=(whole, whole, whole),
        scratch_shapes=[
            vmem((NDP, 2, 2, PAIR, HD), BF16),
            vmem((NH, NX, 2, 4, BLOCK, 2 * HD), BF16),
            vmem((NH, NX, 2, 4, BLOCK, 2 * HD), F32),
            vmem((NDP, 2, PAIR, HD), F32),
            vmem((2, 1, ROWS), jnp.int32),
            vmem((2, 1, ROWS), jnp.int32),
            vmem((3, 2, GROUPS, 1, ROWS), F32),
            vmem((NDP, 8, PAIR), F32),
            vmem((NDP, 8, PAIR), F32),
            vmem((NDP, 8, PAIR), F32),
            vmem((2, GROUPS, 1, ROWS), F32),
            vmem((2, GROUPS, 1, ROWS), F32),
            vmem((NY, 2, PAIR, HD), BF16),
            vmem((NY, 2, PAIR, HD), BF16),
            vmem((2, PAIR, HD), F32),
            vmem((NY - 1, 2, PAIR, HD), BF16),
            vmem((NY - 1, 2, PAIR, HD), BF16),
            vmem((NX - 1, NH, 2, 4, BLOCK, 2 * HD), BF16),
            vmem((NX - 1, NH, 2, 4, BLOCK, 2 * HD), BF16),
            vmem((NH, 2, 4, BLOCK, 2 * HD), F32),
            vmem((16, BLOCK, 2 * HD), BF16),
            vmem((16, BLOCK, 2 * HD), BF16),
            pltpu.SMEM((NDOCS,), jnp.int32),
            pltpu.SemaphoreType.DMA((11,)),
            pltpu.SemaphoreType.DMA((65,)),
            pltpu.SemaphoreType.DMA((65,)),
        ],
        compiler_params=pltpu.CompilerParams(
            collective_id=0, has_side_effects=True, vmem_limit_bytes=60 << 20
        ),
    )(queries, keys, values, out_grads, doc_lengths)


def solution(mesh):
    return jax.shard_map(
        body,
        mesh=mesh,
        in_specs=(P("ctx", "dp"), P("ctx", None), P("ctx", None), P("ctx", "dp"), P()),
        out_specs=(P("ctx", "dp"), P(("ctx", "dp"), None), P(("ctx", "dp"), None)),
        check_vma=False,
    )
```

```python
import jax
import jax.numpy as jnp
from jax import lax
from jax.experimental import pallas as pl
from jax.experimental.pallas import tpu as pltpu
from jax.sharding import PartitionSpec as P

MESH = pl.DeviceIdType.MESH
NH, NX, NZ, NY = 2, 4, 8, 4
NDP = 2 * NY
HD, SPAN, NDOCS = 128, 64, 32
BLOCK = 16
PAIR = 2 * SPAN
ROWS = NDP * PAIR
F_PER, B_PER = 2, 4
TILE = 256
LAST = 127
REACH = 66
LOW, FLOOR = -1e30, -1e29
SCALE = HD**-0.5
LOG2E = 1.4426950408889634
F32, BF16 = jnp.float32, jnp.bfloat16


def dot(a, b, dims):
    return lax.dot_general(a, b, (dims, ((), ())), preferred_element_type=F32)


def kernel(
    q_hbm, k_hbm, v_hbm, g_hbm, lens_hbm,
    dq_hbm, dk_hbm, dv_hbm,
    qg, kv, acc, dqa, qpos, qbeg, run, stat, stat_r, comb, fin, lse, delta,
    dq_sib, dq_sib_r, dq_own, dq_s, dq_r, x_s, x_r, own_x, z_s, z_r,
    dq_out, dk_out, dv_out, lens, loc, send, recv,
):
    ctx, dp = lax.axis_index("ctx"), lax.axis_index("dp")
    h, x, z = lax.div(ctx, 32), lax.rem(lax.div(ctx, 8), 4), lax.rem(ctx, 8)
    y, c = lax.div(dp, 2), lax.rem(dp, 2)
    t, s = lax.div(y, 2), lax.rem(y, 2)
    odd, zh, far = lax.rem(z, 2), lax.div(z, 2), 1 - h
    in_span = BLOCK * (2 * s + c)
    block = 4 * lax.rem(t + z, 2) + 2 * s + c
    across = 4 * (1 - t) + 2 * s + c
    feeder = 6 * (1 - t) + c

    def line(half, dz):
        return half * 32 + x * 8 + lax.rem(z + dz, NZ)

    ys = [(ctx, 2 * lax.rem(y + d, NY) + c) for d in range(1, NY)]
    zs = [(line(h, dz), dp) for dz in range(1, NZ)]
    xs = [(h * 32 + lax.rem(x + d, NX) * 8 + z, dp) for d in range(1, NX)]
    sibling = (ctx, 2 * y + 1 - c)

    sent = []

    def remote(src, dst, n, to, m=None):
        return pltpu.make_async_remote_copy(
            src_ref=src, dst_ref=dst, send_sem=send.at[n], recv_sem=recv.at[n if m is None else m],
            device_id=to, device_id_type=MESH,
        )

    def go(copy):
        copy.start()
        sent.append(copy)
        return copy

    rows = pl.ds(pl.multiple_of(block * BLOCK, BLOCK), BLOCK)
    mine = kv.at[h, x, odd, zh]
    local_kv = [
        pltpu.make_async_copy(k_hbm.at[rows, :], mine.at[:, 0:HD], loc.at[0]),
        pltpu.make_async_copy(v_hbm.at[rows, :], mine.at[:, HD : 2 * HD], loc.at[1]),
    ]
    local_qg = [
        pltpu.make_async_copy(
            ref.at[span * SPAN : (span + 1) * SPAN, head * HD : (head + 1) * HD],
            qg.at[dp, kind, span, head * SPAN : (head + 1) * SPAN, :],
            loc.at[2 + 4 * kind + 2 * span + head],
        )
        for kind, ref in enumerate((q_hbm, g_hbm))
        for span in range(2)
        for head in range(2)
    ]
    local_lens = pltpu.make_async_copy(lens_hbm, lens, loc.at[10])

    barrier = pltpu.get_barrier_semaphore()
    source = jnp.where(odd == 1, across, dp)
    partners = [*zs, *xs, *ys, sibling]
    others = [(line(far, 0), feeder)] + [(line(far, dz), source) for dz in range(NZ)]
    for to in partners + others:
        pl.semaphore_signal(barrier, inc=1, device_id=to, device_id_type=MESH)

    @pl.when(odd == 1)
    def _():
        for to, _ in zs:
            pl.semaphore_signal(barrier, inc=1, device_id=(to, across), device_id_type=MESH)

    for copy in local_kv + local_qg + [local_lens]:
        copy.start()
    pl.semaphore_wait(barrier, len(partners) + NZ + 4 - odd + jnp.where(s == t, 2, 0))

    feed = []
    for to_s in range(2):
        of = 4 * lax.rem(1 - t + z, 2) + 2 * to_s + c
        of_rows = pl.ds(pl.multiple_of(of * BLOCK, BLOCK), BLOCK)
        to = (line(far, 0), 4 * (1 - t) + 2 * to_s + c)
        for kind, ref in enumerate((k_hbm, v_hbm)):
            half = mine.at[:, kind * HD : (kind + 1) * HD]
            feed.append(remote(ref.at[of_rows, :], half, 2 * to_s + kind, to, kind))

    @pl.when(s == t)
    def _():
        for copy in feed:
            copy.start()

    for copy in local_kv:
        copy.wait()
    to_z = [go(remote(mine, mine, 3 + dz, zs[dz - 1])) for dz in range(1, NZ)]
    for copy in local_qg:
        copy.wait()
    own = qg.at[dp]
    to_sib = [go(remote(own, own, 11, sibling))]
    to_y = [go(remote(own, own, 11 + d, ys[d - 1])) for d in range(1, NY)]
    theirs = kv.at[far, x, odd, zh]
    for copy in feed[0:2]:
        copy.wait_recv()
    to_zf = [go(remote(theirs, theirs, 14 + dz, zs[dz - 1])) for dz in range(1, NZ)]
    for copy in to_z:
        copy.wait_recv()
    plane = kv.at[h, x]
    to_x = [go(remote(plane, plane, 21 + d, xs[d - 1])) for d in range(1, NX)]
    for copy in to_zf:
        copy.wait_recv()
    plane_f = kv.at[far, x]
    to_xf = [go(remote(plane_f, plane_f, 24 + d, xs[d - 1])) for d in range(1, NX)]

    local_lens.wait()
    token = lax.rem(lax.broadcasted_iota(jnp.int32, (1, B_PER * PAIR), 1), SPAN)
    for span, first in ((0, ctx * SPAN), (1, (LAST - ctx) * SPAN)):
        pos = first + token
        begin = jnp.zeros_like(pos)
        end = jnp.int32(0)
        for n in range(NDOCS):
            end = end + lens[n]
            begin = jnp.where(pos >= end, end, begin)
        qpos[span] = pos
        qbeg[span] = begin
    run[0] = jnp.full(run.shape[1:], FLOOR, F32)
    run[1] = jnp.zeros(run.shape[1:], F32)
    run[2] = jnp.zeros(run.shape[1:], F32)
    stat[...] = jnp.zeros_like(stat)
    comb[y] = jnp.zeros((NY, 8, PAIR), F32)
    fin[c] = jnp.zeros((NY, 8, PAIR), F32)

    n_tiles = jnp.where((h == 1) | (ctx >= LAST - REACH - 31), 5, 4)
    row = lax.broadcasted_iota(jnp.int32, (TILE, 1), 0)
    row_ctx = 8 * lax.div(row, 64) + 2 * lax.rem(lax.div(row, BLOCK), 4)
    row_in = in_span + lax.rem(row, BLOCK)

    def tile(n, group, per):
        span = jnp.where(n == 0, 1 - h, jnp.where(n == 2, 0, 1))
        half = jnp.where(n == 1, 1 - h, jnp.where(n == 3, 1, 0))
        hi = jnp.where(n < 2, far, h)
        zp = lax.rem(t + half, 2)
        lanes = pl.ds(pl.multiple_of(group * per * PAIR, PAIR), per * PAIR)
        k = kv[hi, :, zp, :, :, 0:HD].reshape(TILE, HD)
        v = kv[hi, :, zp, :, :, HD : 2 * HD].reshape(TILE, HD)
        q = qg[pl.ds(per * group, per), 0, span].reshape(per * PAIR, HD)
        g = qg[pl.ds(per * group, per), 1, span].reshape(per * PAIR, HD)
        of = hi * 32 + zp + row_ctx
        kpos = jnp.where(half == 0, of, LAST - of) * SPAN + row_in
        live = (kpos <= qpos[span, :, 0 : per * PAIR]) & (kpos >= qbeg[span, :, 0 : per * PAIR])
        logits = dot(k, q, ((1,), (1,))) * (SCALE * LOG2E)
        dweights = dot(v, g, ((1,), (1,)))
        return span, lanes, hi, zp, k, q, g, live, logits, dweights

    def forward(group, first, last):
        def step(n, _):
            span, lanes, hi, zp, k, q, g, live, logits, dweights = tile(n, group, F_PER)
            logits = jnp.where(live, logits, LOW)
            old = run[0, span, :, lanes]
            top = jnp.maximum(old, jnp.max(logits, axis=0, keepdims=True))
            terms = jnp.exp2(logits - top)
            keep = jnp.exp2(old - top)
            run[0, span, :, lanes] = top
            run[1, span, :, lanes] = run[1, span, :, lanes] * keep + jnp.sum(terms, axis=0, keepdims=True)
            run[2, span, :, lanes] = run[2, span, :, lanes] * keep + jnp.sum(terms * dweights, axis=0, keepdims=True)
            return 0

        lax.fori_loop(first, last, step, 0)

    def pass_on(d):
        to_y[d - 1].wait_recv()
        got = qg.at[2 * lax.rem(y + NY - d, NY) + c]
        to_sib.append(go(remote(got, got, 27 + d, sibling)))

    to_sib[0].wait_recv()
    for copy in to_x:
        copy.wait_recv()
    forward(y, 2, n_tiles)
    pass_on(1)
    for copy in to_xf:
        copy.wait_recv()
    forward(y, 0, 2)
    pass_on(2)
    to_sib[1].wait_recv()
    forward(lax.rem(y + 3, NY), 0, n_tiles)
    pass_on(3)
    to_sib[2].wait_recv()
    forward(lax.rem(y + 2, NY), 0, n_tiles)
    to_sib[3].wait_recv()
    forward(lax.rem(y + 1, NY), 0, n_tiles)

    for j in range(NDP):
        for kind in range(3):
            for span in range(2):
                n = 2 * kind + span
                stat[j % 2, j // 2, n : n + 1] = run[kind, span, :, j * PAIR : (j + 1) * PAIR]
    to_stat = go(remote(stat.at[1 - c], stat_r, 31, sibling))
    acc[...] = jnp.zeros_like(acc)
    to_stat.wait_recv()

    def merged(parts):
        top = parts[0][:, 0:2]
        for part in parts[1:]:
            top = jnp.maximum(top, part[:, 0:2])
        total, moment = jnp.zeros_like(top), jnp.zeros_like(top)
        for part in parts:
            share = jnp.exp2(part[:, 0:2] - top)
            total = total + share * part[:, 2:4]
            moment = moment + share * part[:, 4:6]
        return top, total, moment

    comb[y, :, 0:2], comb[y, :, 2:4], comb[y, :, 4:6] = merged([stat[c], stat_r[...]])
    to_comb = [go(remote(comb.at[y], comb.at[y], 31 + d, ys[d - 1])) for d in range(1, NY)]
    dqa[...] = jnp.zeros_like(dqa)
    for copy in to_comb:
        copy.wait_recv()
    top, total, moment = merged([comb[n] for n in range(NY)])
    fin[c, :, 0:2] = top + jnp.log(total) * LOG2E
    fin[c, :, 2:4] = moment / total
    to_fin = go(remote(fin.at[c], fin.at[c], 35, sibling))
    to_fin.wait_recv()
    for j in range(NDP):
        for span in range(2):
            lse[span, :, j * PAIR : (j + 1) * PAIR] = fin[j % 2, j // 2, span : span + 1]
            delta[span, :, j * PAIR : (j + 1) * PAIR] = fin[j % 2, j // 2, 2 + span : 3 + span]

    def backward(i, _):
        n, group = lax.div(i, NDP // B_PER), lax.rem(i, NDP // B_PER)
        span, lanes, hi, zp, k, q, g, live, logits, dweights = tile(n, group, B_PER)
        weights = jnp.where(live, jnp.exp2(logits - lse[span, :, lanes]), 0.0)
        dlogits = (weights * (dweights - delta[span, :, lanes])).astype(BF16)
        acc[hi, :, zp, :, :, 0:HD] += dot(dlogits, q, ((1,), (0,))).reshape(NX, 4, BLOCK, HD)
        acc[hi, :, zp, :, :, HD : 2 * HD] += dot(weights.astype(BF16), g, ((1,), (0,))).reshape(NX, 4, BLOCK, HD)
        dqa[pl.ds(B_PER * group, B_PER), span] += dot(dlogits, k, ((0,), (0,))).reshape(B_PER, PAIR, HD)
        return 0

    def over_x(half, at, first):
        copies = []
        for d in range(1, NX):
            x_s[at, d - 1] = acc[half, lax.rem(x + d, NX)].astype(BF16)
            copies.append(go(remote(x_s.at[at, d - 1], x_r.at[at, d - 1], first + d, xs[d - 1])))
        return copies

    lax.fori_loop(0, 2 * (NDP // B_PER), backward, 0)
    to_rxf = over_x(far, 1, 35)
    lax.fori_loop(2 * (NDP // B_PER), n_tiles * (NDP // B_PER), backward, 0)

    to_ds = []
    for n in range(NY):
        of = lax.rem(y + 1 + n, NY)
        dq_sib[n] = dqa[2 * of + 1 - c].astype(BF16)
        to_ds.append(go(remote(dq_sib.at[n], dq_sib_r.at[n], 39 + n, sibling)))
    to_rx = over_x(h, 0, 42)
    to_dq = []
    for n in range(NY):
        of = lax.rem(y + 1 + n, NY)
        to_ds[n].wait_recv()
        both = dqa[2 * of + c] + dq_sib_r[n].astype(F32)
        if n < NY - 1:
            dq_s[n] = both.astype(BF16)
            to_dq.append(go(remote(dq_s.at[n], dq_r.at[n], 46 + n, ys[n])))
        else:
            dq_own[...] = both

    to_rz = []

    def over_z(half, at, copies):
        for copy in copies:
            copy.wait_recv()
        own_x[at] = acc[half, x] + x_r[at, 0].astype(F32) + x_r[at, 1].astype(F32) + x_r[at, 2].astype(F32)
        for dz in range(1 - at, NZ):
            zz = lax.rem(z + dz, NZ)
            n = NZ * at + dz
            z_s[n] = own_x[at, lax.rem(zz, 2), lax.div(zz, 2)].astype(BF16)
            to = (line(half, dz), jnp.where(lax.rem(zz, 2) == 1, across, dp))
            to_rz.append(go(remote(z_s.at[n], z_r.at[n], 49 + n, to)))

    over_z(far, 1, to_rxf)
    over_z(h, 0, to_rx)
    z_s[0] = own_x[0, odd, zh].astype(BF16)
    near = remote(z_s.at[0], z_r.at[0], 49, (ctx, across))

    @pl.when(odd == 1)
    def _():
        near.start()

    @pl.when(odd == 0)
    def _():
        z_r[0] = z_s[0]

    for copy in to_dq:
        copy.wait_recv()
    total_dq = (SCALE * (dq_own[...] + dq_r[0].astype(F32) + dq_r[1].astype(F32) + dq_r[2].astype(F32))).astype(BF16)
    for span in range(2):
        for head in range(2):
            dq_out[span * SPAN : (span + 1) * SPAN, head * HD : (head + 1) * HD] = total_dq[
                span, head * SPAN : (head + 1) * SPAN
            ]
    out_dq = pltpu.make_async_copy(dq_out, dq_hbm, loc.at[0])
    out_dq.start()

    for copy in to_rz:
        copy.wait_recv()

    @pl.when(odd == 1)
    def _():
        near.wait_recv()
        near.wait_send()

    total_kv = z_r[0].astype(F32)
    for n in range(1, 16):
        total_kv = total_kv + z_r[n].astype(F32)
    dk_out[...] = (SCALE * total_kv[:, 0:HD]).astype(BF16)
    dv_out[...] = total_kv[:, HD : 2 * HD].astype(BF16)
    out_dk = pltpu.make_async_copy(dk_out, dk_hbm, loc.at[1])
    out_dv = pltpu.make_async_copy(dv_out, dv_hbm, loc.at[2])
    out_dk.start()
    out_dv.start()

    @pl.when(s == t)
    def _():
        for copy in feed:
            copy.wait_send()

    for copy in sent:
        copy.wait_send()
    for copy in (out_dq, out_dk, out_dv):
        copy.wait()


def hand_on(dq, dk, dv, dq_out, dk_out, dv_out, sem):
    copies = [
        pltpu.make_async_copy(src, dst, sem.at[n])
        for n, (src, dst) in enumerate(((dq, dq_out), (dk, dk_out), (dv, dv_out)))
    ]
    for copy in copies:
        copy.start()
    for copy in copies:
        copy.wait()


def body(queries, keys, values, out_grads, doc_lengths):
    vmem, hbm = pltpu.VMEM, pl.BlockSpec(memory_space=pltpu.HBM)
    shapes = (
        jax.ShapeDtypeStruct(queries.shape, BF16),
        jax.ShapeDtypeStruct((BLOCK, HD), BF16),
        jax.ShapeDtypeStruct((BLOCK, HD), BF16),
    )
    made = pl.pallas_call(
        kernel,
        out_shape=shapes,
        in_specs=[hbm] * 5,
        out_specs=(hbm, hbm, hbm),
        scratch_shapes=[
            vmem((NDP, 2, 2, PAIR, HD), BF16),
            vmem((NH, NX, 2, 4, BLOCK, 2 * HD), BF16),
            vmem((NH, NX, 2, 4, BLOCK, 2 * HD), F32),
            vmem((NDP, 2, PAIR, HD), F32),
            vmem((2, 1, B_PER * PAIR), jnp.int32),
            vmem((2, 1, B_PER * PAIR), jnp.int32),
            vmem((3, 2, 1, ROWS), F32),
            vmem((2, NY, 8, PAIR), F32),
            vmem((NY, 8, PAIR), F32),
            vmem((NY, NY, 8, PAIR), F32),
            vmem((2, NY, 8, PAIR), F32),
            vmem((2, 1, ROWS), F32),
            vmem((2, 1, ROWS), F32),
            vmem((NY, 2, PAIR, HD), BF16),
            vmem((NY, 2, PAIR, HD), BF16),
            vmem((2, PAIR, HD), F32),
            vmem((NY - 1, 2, PAIR, HD), BF16),
            vmem((NY - 1, 2, PAIR, HD), BF16),
            vmem((2, NX - 1, 2, 4, BLOCK, 2 * HD), BF16),
            vmem((2, NX - 1, 2, 4, BLOCK, 2 * HD), BF16),
            vmem((2, 2, 4, BLOCK, 2 * HD), F32),
            vmem((16, BLOCK, 2 * HD), BF16),
            vmem((16, BLOCK, 2 * HD), BF16),
            vmem(queries.shape, BF16),
            vmem((BLOCK, HD), BF16),
            vmem((BLOCK, HD), BF16),
            pltpu.SMEM((NDOCS,), jnp.int32),
            pltpu.SemaphoreType.DMA((11,)),
            pltpu.SemaphoreType.DMA((65,)),
            pltpu.SemaphoreType.DMA((65,)),
        ],
        compiler_params=pltpu.CompilerParams(
            collective_id=0, has_side_effects=True, vmem_limit_bytes=60 << 20
        ),
    )(queries, keys, values, out_grads, doc_lengths)
    return pl.pallas_call(
        hand_on,
        out_shape=shapes,
        in_specs=[hbm] * 3,
        out_specs=(hbm, hbm, hbm),
        scratch_shapes=[pltpu.SemaphoreType.DMA((3,))],
        compiler_params=pltpu.CompilerParams(vmem_limit_bytes=60 << 20),
    )(*made)


def solution(mesh):
    return jax.shard_map(
        body,
        mesh=mesh,
        in_specs=(P("ctx", "dp"), P("ctx", None), P("ctx", None), P("ctx", "dp"), P()),
        out_specs=(P("ctx", "dp"), P(("ctx", "dp"), None), P(("ctx", "dp"), None)),
        check_vma=False,
    )
```

```python
import jax
import jax.numpy as jnp
from jax import lax
from jax.experimental import pallas as pl
from jax.experimental.pallas import tpu as pltpu
from jax.sharding import PartitionSpec as P

MESH = pl.DeviceIdType.MESH
NH, NX, NZ, NY = 2, 4, 8, 4
NDP = 2 * NY
HD, SPAN, NDOCS = 128, 64, 32
BLOCK = 16
PAIR = 2 * SPAN
ROWS = NDP * PAIR
F_PER, B_PER = 2, 4
TILE = 256
LAST = 127
REACH = 66
LOW, FLOOR = -1e30, -1e29
SCALE = HD**-0.5
LOG2E = 1.4426950408889634
F32, BF16 = jnp.float32, jnp.bfloat16


def dot(a, b, dims):
    return lax.dot_general(a, b, (dims, ((), ())), preferred_element_type=F32)


def kernel(
    q_hbm, k_hbm, v_hbm, g_hbm, lens_hbm,
    dq_out, dk_out, dv_out,
    qg, kv, acc, dqa, qpos, qbeg, run, stat, stat_r, comb, fin, lse, delta,
    dq_sib, dq_sib_r, dq_own, dq_s, dq_r, x_s, x_r, own_x, z_s, z_r,
    lens, loc, send, recv,
):
    ctx, dp = lax.axis_index("ctx"), lax.axis_index("dp")
    h, x, z = lax.div(ctx, 32), lax.rem(lax.div(ctx, 8), 4), lax.rem(ctx, 8)
    y, c = lax.div(dp, 2), lax.rem(dp, 2)
    t, s = lax.div(y, 2), lax.rem(y, 2)
    odd, zh, far = lax.rem(z, 2), lax.div(z, 2), 1 - h
    in_span = BLOCK * (2 * s + c)
    block = 4 * lax.rem(t + z, 2) + 2 * s + c
    across = 4 * (1 - t) + 2 * s + c
    feeder = 6 * (1 - t) + c

    def line(half, dz):
        return half * 32 + x * 8 + lax.rem(z + dz, NZ)

    ys = [(ctx, 2 * lax.rem(y + d, NY) + c) for d in range(1, NY)]
    zs = [(line(h, dz), dp) for dz in range(1, NZ)]
    xs = [(h * 32 + lax.rem(x + d, NX) * 8 + z, dp) for d in range(1, NX)]
    sibling = (ctx, 2 * y + 1 - c)

    sent = []

    def remote(src, dst, n, to, m=None):
        return pltpu.make_async_remote_copy(
            src_ref=src, dst_ref=dst, send_sem=send.at[n], recv_sem=recv.at[n if m is None else m],
            device_id=to, device_id_type=MESH,
        )

    def go(copy):
        copy.start()
        sent.append(copy)
        return copy

    rows = pl.ds(pl.multiple_of(block * BLOCK, BLOCK), BLOCK)
    mine = kv.at[h, x, odd, zh]
    local_kv = [
        pltpu.make_async_copy(k_hbm.at[rows, :], mine.at[:, 0:HD], loc.at[0]),
        pltpu.make_async_copy(v_hbm.at[rows, :], mine.at[:, HD : 2 * HD], loc.at[1]),
    ]
    local_qg = [
        pltpu.make_async_copy(
            ref.at[span * SPAN : (span + 1) * SPAN, head * HD : (head + 1) * HD],
            qg.at[dp, span, kind, head * SPAN : (head + 1) * SPAN, :],
            loc.at[2 + 4 * kind + 2 * span + head],
        )
        for kind, ref in enumerate((q_hbm, g_hbm))
        for span in range(2)
        for head in range(2)
    ]
    local_lens = pltpu.make_async_copy(lens_hbm, lens, loc.at[10])

    barrier = pltpu.get_barrier_semaphore()
    source = jnp.where(odd == 1, across, dp)
    partners = [*zs, *xs, *ys, sibling]
    others = [(line(far, 0), feeder)] + [(line(far, dz), source) for dz in range(NZ)]
    for to in partners + others:
        pl.semaphore_signal(barrier, inc=1, device_id=to, device_id_type=MESH)

    @pl.when(odd == 1)
    def _():
        for to, _ in zs:
            pl.semaphore_signal(barrier, inc=1, device_id=(to, across), device_id_type=MESH)

    for copy in local_kv + local_qg + [local_lens]:
        copy.start()
    pl.semaphore_wait(barrier, len(partners) + NZ + 4 - odd + jnp.where(s == t, 2, 0))

    feed = []
    for to_s in range(2):
        of = 4 * lax.rem(1 - t + z, 2) + 2 * to_s + c
        of_rows = pl.ds(pl.multiple_of(of * BLOCK, BLOCK), BLOCK)
        to = (line(far, 0), 4 * (1 - t) + 2 * to_s + c)
        for kind, ref in enumerate((k_hbm, v_hbm)):
            half = mine.at[:, kind * HD : (kind + 1) * HD]
            feed.append(remote(ref.at[of_rows, :], half, 2 * to_s + kind, to, kind))

    @pl.when(s == t)
    def _():
        for copy in feed:
            copy.start()

    for copy in local_kv:
        copy.wait()
    to_z = [go(remote(mine, mine, 3 + dz, zs[dz - 1])) for dz in range(1, NZ)]
    for copy in local_qg:
        copy.wait()
    own = qg.at[dp]
    own_sib = go(remote(own, own, 11, sibling))

    def chip(mask):
        t_to = 1 - t if mask & 2 else t
        return 2 * t_to + (1 - s if mask & 1 else s)

    def piece(of, p):
        return qg.at[2 * of + c, p // 2, p % 2]

    def to_chip(mask, p):
        part = piece(y, p)
        return remote(part, part, 64 + 16 * mask + p, (ctx, 2 * chip(mask) + c), 64 + 4 * mask + p)

    ahead = [[to_chip(mask, p) for mask in (2, 1)] for p in range(4)]
    straight = [to_chip(3, p) for p in range(4)]
    relay = [remote(piece(chip(2), p), piece(chip(2), p), 116 + p, (ctx, 2 * chip(1) + c), 76 + p) for p in range(4)]
    for p in range(4):
        go(ahead[p][0])

        @pl.when(s != t)
        def _():
            straight[p].start()

        go(ahead[p][1])

    to_sib = {}

    def pass_on(p):
        ahead[p][0].wait_recv()

        @pl.when(s != t)
        def _():
            relay[p].start()

        part = piece(chip(2), p)
        to_sib[2, p] = go(remote(part, part, 136 + p, sibling))
        for mask, copy in ((1, ahead[p][1]), (3, straight[p])):
            copy.wait_recv()
            part = piece(chip(mask), p)
            to_sib[mask, p] = go(remote(part, part, 128 + 4 * mask + p, sibling))

    theirs = kv.at[far, x, odd, zh]
    for copy in feed[0:2]:
        copy.wait_recv()
    to_zf = [go(remote(theirs, theirs, 14 + dz, zs[dz - 1])) for dz in range(1, NZ)]
    for copy in to_z:
        copy.wait_recv()
    plane = kv.at[h, x]
    to_x = [go(remote(plane, plane, 21 + d, xs[d - 1])) for d in range(1, NX)]
    for copy in to_zf:
        copy.wait_recv()
    plane_f = kv.at[far, x]
    to_xf = [go(remote(plane_f, plane_f, 24 + d, xs[d - 1])) for d in range(1, NX)]

    pass_on(0)

    local_lens.wait()
    token = lax.rem(lax.broadcasted_iota(jnp.int32, (1, B_PER * PAIR), 1), SPAN)
    for span, first in ((0, ctx * SPAN), (1, (LAST - ctx) * SPAN)):
        pos = first + token
        begin = jnp.zeros_like(pos)
        end = jnp.int32(0)
        for n in range(NDOCS):
            end = end + lens[n]
            begin = jnp.where(pos >= end, end, begin)
        qpos[span] = pos
        qbeg[span] = begin
    run[0] = jnp.full(run.shape[1:], FLOOR, F32)
    run[1] = jnp.zeros(run.shape[1:], F32)
    run[2] = jnp.zeros(run.shape[1:], F32)
    stat[...] = jnp.zeros_like(stat)
    comb[y] = jnp.zeros((NY, 8, PAIR), F32)
    fin[c] = jnp.zeros((NY, 8, PAIR), F32)

    n_tiles = jnp.where((h == 1) | (ctx >= LAST - REACH - 31), 5, 4)
    row = lax.broadcasted_iota(jnp.int32, (TILE, 1), 0)
    row_ctx = 8 * lax.div(row, 64) + 2 * lax.rem(lax.div(row, BLOCK), 4)
    row_in = in_span + lax.rem(row, BLOCK)

    def tile(n, group, per):
        span = jnp.where(n == 0, 1 - h, jnp.where(n == 2, 0, 1))
        half = jnp.where(n == 1, 1 - h, jnp.where(n == 3, 1, 0))
        hi = jnp.where(n < 2, far, h)
        zp = lax.rem(t + half, 2)
        lanes = pl.ds(pl.multiple_of(group * per * PAIR, PAIR), per * PAIR)
        k = kv[hi, :, zp, :, :, 0:HD].reshape(TILE, HD)
        v = kv[hi, :, zp, :, :, HD : 2 * HD].reshape(TILE, HD)
        q = qg[pl.ds(per * group, per), span, 0].reshape(per * PAIR, HD)
        g = qg[pl.ds(per * group, per), span, 1].reshape(per * PAIR, HD)
        of = hi * 32 + zp + row_ctx
        kpos = jnp.where(half == 0, of, LAST - of) * SPAN + row_in
        live = (kpos <= qpos[span, :, 0 : per * PAIR]) & (kpos >= qbeg[span, :, 0 : per * PAIR])
        logits = dot(k, q, ((1,), (1,))) * (SCALE * LOG2E)
        dweights = dot(v, g, ((1,), (1,)))
        return span, lanes, hi, zp, k, q, g, live, logits, dweights

    def forward(group, first, last):
        def step(n, _):
            span, lanes, hi, zp, k, q, g, live, logits, dweights = tile(n, group, F_PER)
            logits = jnp.where(live, logits, LOW)
            old = run[0, span, :, lanes]
            top = jnp.maximum(old, jnp.max(logits, axis=0, keepdims=True))
            terms = jnp.exp2(logits - top)
            keep = jnp.exp2(old - top)
            run[0, span, :, lanes] = top
            run[1, span, :, lanes] = run[1, span, :, lanes] * keep + jnp.sum(terms, axis=0, keepdims=True)
            run[2, span, :, lanes] = run[2, span, :, lanes] * keep + jnp.sum(terms * dweights, axis=0, keepdims=True)
            return 0

        lax.fori_loop(first, last, step, 0)

    own_sib.wait_recv()
    for copy in to_x:
        copy.wait_recv()
    forward(y, 2, n_tiles)
    pass_on(1)
    for copy in to_xf:
        copy.wait_recv()
    forward(y, 0, 2)
    pass_on(2)
    pass_on(3)
    for mask in (2, 1, 3):
        for p in range(4):
            to_sib[mask, p].wait_recv()
        forward(chip(mask), 0, n_tiles)

    for j in range(NDP):
        for kind in range(3):
            for span in range(2):
                n = 2 * kind + span
                stat[j % 2, j // 2, n : n + 1] = run[kind, span, :, j * PAIR : (j + 1) * PAIR]
    to_stat = go(remote(stat.at[1 - c], stat_r, 31, sibling))
    acc[...] = jnp.zeros_like(acc)
    to_stat.wait_recv()

    def merged(parts):
        top = parts[0][:, 0:2]
        for part in parts[1:]:
            top = jnp.maximum(top, part[:, 0:2])
        total, moment = jnp.zeros_like(top), jnp.zeros_like(top)
        for part in parts:
            share = jnp.exp2(part[:, 0:2] - top)
            total = total + share * part[:, 2:4]
            moment = moment + share * part[:, 4:6]
        return top, total, moment

    comb[y, :, 0:2], comb[y, :, 2:4], comb[y, :, 4:6] = merged([stat[c], stat_r[...]])
    to_comb = [go(remote(comb.at[y], comb.at[y], 31 + d, ys[d - 1])) for d in range(1, NY)]
    dqa[...] = jnp.zeros_like(dqa)
    for copy in to_comb:
        copy.wait_recv()
    top, total, moment = merged([comb[n] for n in range(NY)])
    fin[c, :, 0:2] = top + jnp.log(total) * LOG2E
    fin[c, :, 2:4] = moment / total
    to_fin = go(remote(fin.at[c], fin.at[c], 35, sibling))
    to_fin.wait_recv()
    for j in range(NDP):
        for span in range(2):
            lse[span, :, j * PAIR : (j + 1) * PAIR] = fin[j % 2, j // 2, span : span + 1]
            delta[span, :, j * PAIR : (j + 1) * PAIR] = fin[j % 2, j // 2, 2 + span : 3 + span]

    def backward(n, group):
        span, lanes, hi, zp, k, q, g, live, logits, dweights = tile(n, group, B_PER)
        weights = jnp.where(live, jnp.exp2(logits - lse[span, :, lanes]), 0.0)
        dlogits = (weights * (dweights - delta[span, :, lanes])).astype(BF16)
        acc[hi, :, zp, :, :, 0:HD] += dot(dlogits, q, ((1,), (0,))).reshape(NX, 4, BLOCK, HD)
        acc[hi, :, zp, :, :, HD : 2 * HD] += dot(weights.astype(BF16), g, ((1,), (0,))).reshape(NX, 4, BLOCK, HD)
        dqa[pl.ds(B_PER * group, B_PER), span] += dot(dlogits, k, ((0,), (0,))).reshape(B_PER, PAIR, HD)
        return group

    def over_x(half, at, first):
        copies = []
        for d in range(1, NX):
            x_s[at, d - 1] = acc[half, lax.rem(x + d, NX)].astype(BF16)
            copies.append(go(remote(x_s.at[at, d - 1], x_r.at[at, d - 1], first + d, xs[d - 1])))
        return copies

    def far_tiles(i, _):
        backward(lax.div(i, 2), lax.rem(i, 2))
        return 0

    lax.fori_loop(0, 4, far_tiles, 0)
    to_rxf = over_x(far, 1, 35)

    def to_core(mask):
        dq_sib[mask] = dqa[2 * chip(mask) + 1 - c].astype(BF16)
        return go(remote(dq_sib.at[mask], dq_sib_r.at[mask], 39 + mask, sibling))

    def from_core(mask, copy):
        copy.wait_recv()
        return dqa[2 * chip(mask) + c] + dq_sib_r[mask].astype(F32)

    def over_chips(mask, copy):
        dq_s[mask - 1] = from_core(mask, copy).astype(BF16)
        return go(remote(dq_s.at[mask - 1], dq_r.at[mask - 1], 45 + mask, (ctx, 2 * chip(mask) + c)))

    lax.fori_loop(2, n_tiles, backward, 1 - t)
    to_ds = {mask: to_core(mask) for mask in (3, 2)}
    lax.fori_loop(2, n_tiles, backward, t)
    to_ds.update({mask: to_core(mask) for mask in (1, 0)})
    to_rx = over_x(h, 0, 42)
    to_dq = [over_chips(mask, to_ds[mask]) for mask in (3, 2, 1)]
    dq_own[...] = from_core(0, to_ds[0])

    to_rz = []

    def over_z(half, at, copies):
        for copy in copies:
            copy.wait_recv()
        own_x[at] = acc[half, x] + x_r[at, 0].astype(F32) + x_r[at, 1].astype(F32) + x_r[at, 2].astype(F32)
        for dz in range(1 - at, NZ):
            zz = lax.rem(z + dz, NZ)
            n = NZ * at + dz
            z_s[n] = own_x[at, lax.rem(zz, 2), lax.div(zz, 2)].astype(BF16)
            to = (line(half, dz), jnp.where(lax.rem(zz, 2) == 1, across, dp))
            to_rz.append(go(remote(z_s.at[n], z_r.at[n], 49 + n, to)))

    over_z(far, 1, to_rxf)
    over_z(h, 0, to_rx)
    z_s[0] = own_x[0, odd, zh].astype(BF16)
    near = remote(z_s.at[0], z_r.at[0], 49, (ctx, across))

    @pl.when(odd == 1)
    def _():
        near.start()

    @pl.when(odd == 0)
    def _():
        z_r[0] = z_s[0]

    for copy in to_dq:
        copy.wait_recv()
    total_dq = (SCALE * (dq_own[...] + dq_r[0].astype(F32) + dq_r[1].astype(F32) + dq_r[2].astype(F32))).astype(BF16)
    for span in range(2):
        for head in range(2):
            dq_out[span * SPAN : (span + 1) * SPAN, head * HD : (head + 1) * HD] = total_dq[
                span, head * SPAN : (head + 1) * SPAN
            ]

    for copy in to_rz:
        copy.wait_recv()

    @pl.when(odd == 1)
    def _():
        near.wait_recv()
        near.wait_send()

    total_kv = z_r[0].astype(F32)
    for n in range(1, 16):
        total_kv = total_kv + z_r[n].astype(F32)
    dk_out[...] = (SCALE * total_kv[:, 0:HD]).astype(BF16)
    dv_out[...] = total_kv[:, HD : 2 * HD].astype(BF16)

    @pl.when(s == t)
    def _():
        for copy in feed:
            copy.wait_send()

    @pl.when(s != t)
    def _():
        for copy in straight + relay:
            copy.wait_send()

    for copy in sent:
        copy.wait_send()


def hand_on(dq, dk, dv, dq_out, dk_out, dv_out, sem):
    copies = [
        pltpu.make_async_copy(src, dst, sem.at[n])
        for n, (src, dst) in enumerate(((dq, dq_out), (dk, dk_out), (dv, dv_out)))
    ]
    for copy in copies:
        copy.start()
    for copy in copies:
        copy.wait()


def body(queries, keys, values, out_grads, doc_lengths):
    vmem, hbm = pltpu.VMEM, pl.BlockSpec(memory_space=pltpu.HBM)
    whole = pl.BlockSpec(memory_space=pltpu.VMEM)
    shapes = (
        jax.ShapeDtypeStruct(queries.shape, BF16),
        jax.ShapeDtypeStruct((BLOCK, HD), BF16),
        jax.ShapeDtypeStruct((BLOCK, HD), BF16),
    )
    ins = [
        pltpu.with_memory_space_constraint(a, pltpu.HBM)
        for a in (queries, keys, values, out_grads, doc_lengths)
    ]
    made = pl.pallas_call(
        kernel,
        out_shape=shapes,
        in_specs=[hbm] * 5,
        out_specs=(whole, whole, whole),
        scratch_shapes=[
            vmem((NDP, 2, 2, PAIR, HD), BF16),
            vmem((NH, NX, 2, 4, BLOCK, 2 * HD), BF16),
            vmem((NH, NX, 2, 4, BLOCK, 2 * HD), F32),
            vmem((NDP, 2, PAIR, HD), F32),
            vmem((2, 1, B_PER * PAIR), jnp.int32),
            vmem((2, 1, B_PER * PAIR), jnp.int32),
            vmem((3, 2, 1, ROWS), F32),
            vmem((2, NY, 8, PAIR), F32),
            vmem((NY, 8, PAIR), F32),
            vmem((NY, NY, 8, PAIR), F32),
            vmem((2, NY, 8, PAIR), F32),
            vmem((2, 1, ROWS), F32),
            vmem((2, 1, ROWS), F32),
            vmem((NY, 2, PAIR, HD), BF16),
            vmem((NY, 2, PAIR, HD), BF16),
            vmem((2, PAIR, HD), F32),
            vmem((NY - 1, 2, PAIR, HD), BF16),
            vmem((NY - 1, 2, PAIR, HD), BF16),
            vmem((2, NX - 1, 2, 4, BLOCK, 2 * HD), BF16),
            vmem((2, NX - 1, 2, 4, BLOCK, 2 * HD), BF16),
            vmem((2, 2, 4, BLOCK, 2 * HD), F32),
            vmem((16, BLOCK, 2 * HD), BF16),
            vmem((16, BLOCK, 2 * HD), BF16),
            pltpu.SMEM((NDOCS,), jnp.int32),
            pltpu.SemaphoreType.DMA((11,)),
            pltpu.SemaphoreType.DMA((144,)),
            pltpu.SemaphoreType.DMA((144,)),
        ],
        compiler_params=pltpu.CompilerParams(
            collective_id=0, has_side_effects=True, vmem_limit_bytes=40 << 20
        ),
    )(*ins)
    return pl.pallas_call(
        hand_on,
        out_shape=shapes,
        in_specs=[whole] * 3,
        out_specs=(hbm, hbm, hbm),
        scratch_shapes=[pltpu.SemaphoreType.DMA((3,))],
        compiler_params=pltpu.CompilerParams(vmem_limit_bytes=16 << 20),
    )(*made)


def solution(mesh):
    return jax.shard_map(
        body,
        mesh=mesh,
        in_specs=(P("ctx", "dp"), P("ctx", None), P("ctx", None), P("ctx", "dp"), P()),
        out_specs=(P("ctx", "dp"), P(("ctx", "dp"), None), P(("ctx", "dp"), None)),
        check_vma=False,
    )
```

```python
import jax
import jax.numpy as jnp
from jax import lax
from jax.experimental import pallas as pl
from jax.experimental.pallas import tpu as pltpu
from jax.sharding import PartitionSpec as P

MESH = pl.DeviceIdType.MESH
NH, NX, NZ, NY = 2, 4, 8, 4
NDP = 2 * NY
HD, SPAN, NDOCS = 128, 64, 32
BLOCK = 16
PAIR = 2 * SPAN
ROWS = NDP * PAIR
F_PER, B_PER = 2, 4
TILE = 256
LAST = 127
REACH = 66
LOW, FLOOR = -1e30, -1e29
SCALE = HD**-0.5
LOG2E = 1.4426950408889634
F32, BF16 = jnp.float32, jnp.bfloat16


def dot(a, b, dims):
    return lax.dot_general(a, b, (dims, ((), ())), preferred_element_type=F32)


def kernel(
    q_hbm, k_hbm, v_hbm, g_hbm, lens_hbm,
    dq_out, dk_out, dv_out,
    qg, kv, acc, dqa, qpos, qbeg, run, stat, stat_r, comb, fin, lse, delta,
    dq_sib, dq_sib_r, dq_own, dq_s, dq_r, x_s, x_r, own_x, z_s, z_r,
    lens, loc, send, recv,
):
    ctx, dp = lax.axis_index("ctx"), lax.axis_index("dp")
    h, x, z = lax.div(ctx, 32), lax.rem(lax.div(ctx, 8), 4), lax.rem(ctx, 8)
    y, c = lax.div(dp, 2), lax.rem(dp, 2)
    t, s = lax.div(y, 2), lax.rem(y, 2)
    odd, zh, far = lax.rem(z, 2), lax.div(z, 2), 1 - h
    in_span = BLOCK * (2 * s + c)
    block = 4 * lax.rem(t + z, 2) + 2 * s + c
    across = 4 * (1 - t) + 2 * s + c
    feeder = 6 * (1 - t) + c

    def line(half, dz):
        return half * 32 + x * 8 + lax.rem(z + dz, NZ)

    ys = [(ctx, 2 * lax.rem(y + d, NY) + c) for d in range(1, NY)]
    zs = [(line(h, dz), dp) for dz in range(1, NZ)]
    xs = [(h * 32 + lax.rem(x + d, NX) * 8 + z, dp) for d in range(1, NX)]
    sibling = (ctx, 2 * y + 1 - c)

    def chip(mask):
        t_to = 1 - t if mask & 2 else t
        return 2 * t_to + (1 - s if mask & 1 else s)

    sent = []

    def remote(src, dst, n, to, m=None):
        return pltpu.make_async_remote_copy(
            src_ref=src, dst_ref=dst, send_sem=send.at[n], recv_sem=recv.at[n if m is None else m],
            device_id=to, device_id_type=MESH,
        )

    def go(copy):
        copy.start()
        sent.append(copy)
        return copy

    rows = pl.ds(pl.multiple_of(block * BLOCK, BLOCK), BLOCK)
    mine = kv.at[h, x, odd, zh]
    local_kv = [
        pltpu.make_async_copy(k_hbm.at[rows, :], mine.at[:, 0:HD], loc.at[0]),
        pltpu.make_async_copy(v_hbm.at[rows, :], mine.at[:, HD : 2 * HD], loc.at[1]),
    ]
    local_qg = [
        pltpu.make_async_copy(
            ref.at[span * SPAN : (span + 1) * SPAN, head * HD : (head + 1) * HD],
            qg.at[dp, kind, span, head * SPAN : (head + 1) * SPAN, :],
            loc.at[2 + 4 * kind + 2 * span + head],
        )
        for kind, ref in enumerate((q_hbm, g_hbm))
        for span in range(2)
        for head in range(2)
    ]
    local_lens = pltpu.make_async_copy(lens_hbm, lens, loc.at[10])

    barrier = pltpu.get_barrier_semaphore()
    source = jnp.where(odd == 1, across, dp)
    partners = [*zs, *xs, *ys, sibling]
    others = [(line(far, 0), feeder)] + [(line(far, dz), source) for dz in range(NZ)]
    for to in partners + others:
        pl.semaphore_signal(barrier, inc=1, device_id=to, device_id_type=MESH)

    @pl.when(odd == 1)
    def _():
        for to, _ in zs:
            pl.semaphore_signal(barrier, inc=1, device_id=(to, across), device_id_type=MESH)

    for copy in local_kv + local_qg + [local_lens]:
        copy.start()
    pl.semaphore_wait(barrier, len(partners) + NZ + 4 - odd + jnp.where(s == t, 2, 0))

    feed = []
    for to_s in range(2):
        of = 4 * lax.rem(1 - t + z, 2) + 2 * to_s + c
        of_rows = pl.ds(pl.multiple_of(of * BLOCK, BLOCK), BLOCK)
        to = (line(far, 0), 4 * (1 - t) + 2 * to_s + c)
        for kind, ref in enumerate((k_hbm, v_hbm)):
            half = mine.at[:, kind * HD : (kind + 1) * HD]
            feed.append(remote(ref.at[of_rows, :], half, 2 * to_s + kind, to, kind))

    for copy in local_qg:
        copy.wait()
    own = qg.at[dp]
    to_y = {mask: go(remote(own, own, 11 + mask, (ctx, 2 * chip(mask) + c))) for mask in (2, 3, 1)}

    @pl.when(s == t)
    def _():
        for copy in feed:
            copy.start()

    for copy in local_kv:
        copy.wait()
    to_z = [go(remote(mine, mine, 3 + dz, zs[dz - 1])) for dz in range(1, NZ)]
    to_sib = {0: go(remote(own, own, 11, sibling))}
    theirs = kv.at[far, x, odd, zh]
    for copy in feed[0:2]:
        copy.wait_recv()
    to_zf = [go(remote(theirs, theirs, 14 + dz, zs[dz - 1])) for dz in range(1, NZ)]
    for copy in to_z:
        copy.wait_recv()
    plane = kv.at[h, x]
    to_x = [go(remote(plane, plane, 21 + d, xs[d - 1])) for d in range(1, NX)]
    for copy in to_zf:
        copy.wait_recv()
    plane_f = kv.at[far, x]
    to_xf = [go(remote(plane_f, plane_f, 24 + d, xs[d - 1])) for d in range(1, NX)]

    local_lens.wait()
    token = lax.rem(lax.broadcasted_iota(jnp.int32, (1, B_PER * PAIR), 1), SPAN)
    for span, first in ((0, ctx * SPAN), (1, (LAST - ctx) * SPAN)):
        pos = first + token
        begin = jnp.zeros_like(pos)
        end = jnp.int32(0)
        for n in range(NDOCS):
            end = end + lens[n]
            begin = jnp.where(pos >= end, end, begin)
        qpos[span] = pos
        qbeg[span] = begin
    run[0] = jnp.full(run.shape[1:], FLOOR, F32)
    run[1] = jnp.zeros(run.shape[1:], F32)
    run[2] = jnp.zeros(run.shape[1:], F32)
    stat[...] = jnp.zeros_like(stat)
    comb[y] = jnp.zeros((NY, 8, PAIR), F32)
    fin[c] = jnp.zeros((NY, 8, PAIR), F32)

    n_tiles = jnp.where((h == 1) | (ctx >= LAST - REACH - 31), 5, 4)
    row = lax.broadcasted_iota(jnp.int32, (TILE, 1), 0)
    row_ctx = 8 * lax.div(row, 64) + 2 * lax.rem(lax.div(row, BLOCK), 4)
    row_in = in_span + lax.rem(row, BLOCK)

    def tile(n, group, per):
        span = jnp.where(n == 0, 1 - h, jnp.where(n == 2, 0, 1))
        half = jnp.where(n == 1, 1 - h, jnp.where(n == 3, 1, 0))
        hi = jnp.where(n < 2, far, h)
        zp = lax.rem(t + half, 2)
        lanes = pl.ds(pl.multiple_of(group * per * PAIR, PAIR), per * PAIR)
        k = kv[hi, :, zp, :, :, 0:HD].reshape(TILE, HD)
        v = kv[hi, :, zp, :, :, HD : 2 * HD].reshape(TILE, HD)
        q = qg[pl.ds(per * group, per), 0, span].reshape(per * PAIR, HD)
        g = qg[pl.ds(per * group, per), 1, span].reshape(per * PAIR, HD)
        of = hi * 32 + zp + row_ctx
        kpos = jnp.where(half == 0, of, LAST - of) * SPAN + row_in
        live = (kpos <= qpos[span, :, 0 : per * PAIR]) & (kpos >= qbeg[span, :, 0 : per * PAIR])
        logits = dot(k, q, ((1,), (1,))) * (SCALE * LOG2E)
        dweights = dot(v, g, ((1,), (1,)))
        return span, lanes, hi, zp, k, q, g, live, logits, dweights

    def forward(group, first, last):
        def step(n, _):
            span, lanes, hi, zp, k, q, g, live, logits, dweights = tile(n, group, F_PER)
            logits = jnp.where(live, logits, LOW)
            old = run[0, span, :, lanes]
            top = jnp.maximum(old, jnp.max(logits, axis=0, keepdims=True))
            terms = jnp.exp2(logits - top)
            keep = jnp.exp2(old - top)
            run[0, span, :, lanes] = top
            run[1, span, :, lanes] = run[1, span, :, lanes] * keep + jnp.sum(terms, axis=0, keepdims=True)
            run[2, span, :, lanes] = run[2, span, :, lanes] * keep + jnp.sum(terms * dweights, axis=0, keepdims=True)
            return 0

        lax.fori_loop(first, last, step, 0)

    def pass_on(mask):
        to_y[mask].wait_recv()
        got = qg.at[2 * chip(mask) + c]
        to_sib[mask] = go(remote(got, got, 27 + mask, sibling))

    to_sib[0].wait_recv()
    for copy in to_x:
        copy.wait_recv()
    forward(y, 2, n_tiles)
    pass_on(1)
    for copy in to_xf:
        copy.wait_recv()
    forward(y, 0, 2)
    to_sib[1].wait_recv()
    forward(chip(1), 0, n_tiles)
    pass_on(2)
    pass_on(3)
    for mask in (2, 3):
        to_sib[mask].wait_recv()
        forward(chip(mask), 0, n_tiles)

    for j in range(NDP):
        for kind in range(3):
            for span in range(2):
                n = 2 * kind + span
                stat[j % 2, j // 2, n : n + 1] = run[kind, span, :, j * PAIR : (j + 1) * PAIR]
    to_stat = go(remote(stat.at[1 - c], stat_r, 31, sibling))
    acc[...] = jnp.zeros_like(acc)
    to_stat.wait_recv()

    def merged(parts):
        top = parts[0][:, 0:2]
        for part in parts[1:]:
            top = jnp.maximum(top, part[:, 0:2])
        total, moment = jnp.zeros_like(top), jnp.zeros_like(top)
        for part in parts:
            share = jnp.exp2(part[:, 0:2] - top)
            total = total + share * part[:, 2:4]
            moment = moment + share * part[:, 4:6]
        return top, total, moment

    comb[y, :, 0:2], comb[y, :, 2:4], comb[y, :, 4:6] = merged([stat[c], stat_r[...]])
    to_comb = [go(remote(comb.at[y], comb.at[y], 31 + d, ys[d - 1])) for d in range(1, NY)]
    dqa[...] = jnp.zeros_like(dqa)
    for copy in to_comb:
        copy.wait_recv()
    top, total, moment = merged([comb[n] for n in range(NY)])
    fin[c, :, 0:2] = top + jnp.log(total) * LOG2E
    fin[c, :, 2:4] = moment / total
    to_fin = go(remote(fin.at[c], fin.at[c], 35, sibling))
    to_fin.wait_recv()
    for j in range(NDP):
        for span in range(2):
            lse[span, :, j * PAIR : (j + 1) * PAIR] = fin[j % 2, j // 2, span : span + 1]
            delta[span, :, j * PAIR : (j + 1) * PAIR] = fin[j % 2, j // 2, 2 + span : 3 + span]

    def backward(n, group):
        span, lanes, hi, zp, k, q, g, live, logits, dweights = tile(n, group, B_PER)
        weights = jnp.where(live, jnp.exp2(logits - lse[span, :, lanes]), 0.0)
        dlogits = (weights * (dweights - delta[span, :, lanes])).astype(BF16)
        acc[hi, :, zp, :, :, 0:HD] += dot(dlogits, q, ((1,), (0,))).reshape(NX, 4, BLOCK, HD)
        acc[hi, :, zp, :, :, HD : 2 * HD] += dot(weights.astype(BF16), g, ((1,), (0,))).reshape(NX, 4, BLOCK, HD)
        dqa[pl.ds(B_PER * group, B_PER), span] += dot(dlogits, k, ((0,), (0,))).reshape(B_PER, PAIR, HD)
        return group

    def over_x(half, at, first):
        copies = []
        for d in range(1, NX):
            x_s[at, d - 1] = acc[half, lax.rem(x + d, NX)].astype(BF16)
            copies.append(go(remote(x_s.at[at, d - 1], x_r.at[at, d - 1], first + d, xs[d - 1])))
        return copies

    def far_tiles(i, _):
        backward(lax.div(i, 2), lax.rem(i, 2))
        return 0

    lax.fori_loop(0, 4, far_tiles, 0)
    to_rxf = over_x(far, 1, 35)

    def to_core(mask):
        dq_sib[mask] = dqa[2 * chip(mask) + 1 - c].astype(BF16)
        return go(remote(dq_sib.at[mask], dq_sib_r.at[mask], 39 + mask, sibling))

    def from_core(mask, copy):
        copy.wait_recv()
        return dqa[2 * chip(mask) + c] + dq_sib_r[mask].astype(F32)

    def over_chips(mask, copy):
        dq_s[mask - 1] = from_core(mask, copy).astype(BF16)
        return go(remote(dq_s.at[mask - 1], dq_r.at[mask - 1], 45 + mask, (ctx, 2 * chip(mask) + c)))

    lax.fori_loop(2, n_tiles, backward, 1 - t)
    to_ds = {mask: to_core(mask) for mask in (3, 2)}
    lax.fori_loop(2, n_tiles, backward, t)
    to_rx = over_x(h, 0, 42)
    to_dq = [over_chips(mask, to_ds[mask]) for mask in (3, 2)]
    to_ds.update({mask: to_core(mask) for mask in (1, 0)})
    to_rz = []

    def over_z(half, at, copies):
        for copy in copies:
            copy.wait_recv()
        own_x[at] = acc[half, x] + x_r[at, 0].astype(F32) + x_r[at, 1].astype(F32) + x_r[at, 2].astype(F32)
        for dz in range(1 - at, NZ):
            zz = lax.rem(z + dz, NZ)
            n = NZ * at + dz
            z_s[n] = own_x[at, lax.rem(zz, 2), lax.div(zz, 2)].astype(BF16)
            to = (line(half, dz), jnp.where(lax.rem(zz, 2) == 1, across, dp))
            to_rz.append(go(remote(z_s.at[n], z_r.at[n], 49 + n, to)))

    over_z(far, 1, to_rxf)
    to_dq.append(over_chips(1, to_ds[1]))
    dq_own[...] = from_core(0, to_ds[0])

    over_z(h, 0, to_rx)
    z_s[0] = own_x[0, odd, zh].astype(BF16)
    near = remote(z_s.at[0], z_r.at[0], 49, (ctx, across))

    @pl.when(odd == 1)
    def _():
        near.start()

    @pl.when(odd == 0)
    def _():
        z_r[0] = z_s[0]

    for copy in to_dq:
        copy.wait_recv()
    total_dq = (SCALE * (dq_own[...] + dq_r[0].astype(F32) + dq_r[1].astype(F32) + dq_r[2].astype(F32))).astype(BF16)
    for span in range(2):
        for head in range(2):
            dq_out[span * SPAN : (span + 1) * SPAN, head * HD : (head + 1) * HD] = total_dq[
                span, head * SPAN : (head + 1) * SPAN
            ]

    for copy in to_rz:
        copy.wait_recv()

    @pl.when(odd == 1)
    def _():
        near.wait_recv()
        near.wait_send()

    total_kv = z_r[0].astype(F32)
    for n in range(1, 16):
        total_kv = total_kv + z_r[n].astype(F32)
    dk_out[...] = (SCALE * total_kv[:, 0:HD]).astype(BF16)
    dv_out[...] = total_kv[:, HD : 2 * HD].astype(BF16)

    @pl.when(s == t)
    def _():
        for copy in feed:
            copy.wait_send()

    for copy in sent:
        copy.wait_send()


def hand_on(dq, dk, dv, dq_out, dk_out, dv_out, sem):
    copies = [
        pltpu.make_async_copy(src, dst, sem.at[n])
        for n, (src, dst) in enumerate(((dq, dq_out), (dk, dk_out), (dv, dv_out)))
    ]
    for copy in copies:
        copy.start()
    for copy in copies:
        copy.wait()


def body(queries, keys, values, out_grads, doc_lengths):
    vmem, hbm = pltpu.VMEM, pl.BlockSpec(memory_space=pltpu.HBM)
    whole = pl.BlockSpec(memory_space=pltpu.VMEM)
    shapes = (
        jax.ShapeDtypeStruct(queries.shape, BF16),
        jax.ShapeDtypeStruct((BLOCK, HD), BF16),
        jax.ShapeDtypeStruct((BLOCK, HD), BF16),
    )
    ins = [
        pltpu.with_memory_space_constraint(a, pltpu.HBM)
        for a in (queries, keys, values, out_grads, doc_lengths)
    ]
    made = pl.pallas_call(
        kernel,
        out_shape=shapes,
        in_specs=[hbm] * 5,
        out_specs=(whole, whole, whole),
        scratch_shapes=[
            vmem((NDP, 2, 2, PAIR, HD), BF16),
            vmem((NH, NX, 2, 4, BLOCK, 2 * HD), BF16),
            vmem((NH, NX, 2, 4, BLOCK, 2 * HD), F32),
            vmem((NDP, 2, PAIR, HD), F32),
            vmem((2, 1, B_PER * PAIR), jnp.int32),
            vmem((2, 1, B_PER * PAIR), jnp.int32),
            vmem((3, 2, 1, ROWS), F32),
            vmem((2, NY, 8, PAIR), F32),
            vmem((NY, 8, PAIR), F32),
            vmem((NY, NY, 8, PAIR), F32),
            vmem((2, NY, 8, PAIR), F32),
            vmem((2, 1, ROWS), F32),
            vmem((2, 1, ROWS), F32),
            vmem((NY, 2, PAIR, HD), BF16),
            vmem((NY, 2, PAIR, HD), BF16),
            vmem((2, PAIR, HD), F32),
            vmem((NY - 1, 2, PAIR, HD), BF16),
            vmem((NY - 1, 2, PAIR, HD), BF16),
            vmem((2, NX - 1, 2, 4, BLOCK, 2 * HD), BF16),
            vmem((2, NX - 1, 2, 4, BLOCK, 2 * HD), BF16),
            vmem((2, 2, 4, BLOCK, 2 * HD), F32),
            vmem((16, BLOCK, 2 * HD), BF16),
            vmem((16, BLOCK, 2 * HD), BF16),
            pltpu.SMEM((NDOCS,), jnp.int32),
            pltpu.SemaphoreType.DMA((11,)),
            pltpu.SemaphoreType.DMA((65,)),
            pltpu.SemaphoreType.DMA((65,)),
        ],
        compiler_params=pltpu.CompilerParams(
            collective_id=0, has_side_effects=True, vmem_limit_bytes=40 << 20
        ),
    )(*ins)
    return pl.pallas_call(
        hand_on,
        out_shape=shapes,
        in_specs=[whole] * 3,
        out_specs=(hbm, hbm, hbm),
        scratch_shapes=[pltpu.SemaphoreType.DMA((3,))],
        compiler_params=pltpu.CompilerParams(vmem_limit_bytes=16 << 20),
    )(*made)


def solution(mesh):
    return jax.shard_map(
        body,
        mesh=mesh,
        in_specs=(P("ctx", "dp"), P("ctx", None), P("ctx", None), P("ctx", "dp"), P()),
        out_specs=(P("ctx", "dp"), P(("ctx", "dp"), None), P(("ctx", "dp"), None)),
        check_vma=False,
    )
```

```python
import jax
import jax.numpy as jnp
from jax import lax
from jax.experimental import pallas as pl
from jax.experimental.pallas import tpu as pltpu
from jax.sharding import PartitionSpec as P

MESH = pl.DeviceIdType.MESH
NH, NX, NZ, NY = 2, 4, 8, 4
NDP = 2 * NY
HD, SPAN, NDOCS = 128, 64, 32
BLOCK = 16
PAIR = 2 * SPAN
ROWS = NDP * PAIR
PER = 4
TILE = 256
LAST = 127
REACH = 66
LOW, FLOOR = -1e30, -1e29
SCALE = HD**-0.5
LOG2E = 1.4426950408889634
F32, BF16 = jnp.float32, jnp.bfloat16


def dot(a, b, dims):
    return lax.dot_general(a, b, (dims, ((), ())), preferred_element_type=F32)


def kernel(
    q_hbm, k_hbm, v_hbm, g_hbm, lens_hbm,
    dq_out, dk_out, dv_out,
    qg, kv, acc, dqa, qpos, qbeg, kept, tops, run, stat, stat_r, comb, fin, lse, delta,
    dq_sib, dq_sib_r, dq_own, dq_s, dq_r, x_s, x_r, own_x, z_s, z_r,
    lens, loc, send, recv,
):
    ctx, dp = lax.axis_index("ctx"), lax.axis_index("dp")
    h, x, z = lax.div(ctx, 32), lax.rem(lax.div(ctx, 8), 4), lax.rem(ctx, 8)
    y, c = lax.div(dp, 2), lax.rem(dp, 2)
    t, s = lax.div(y, 2), lax.rem(y, 2)
    odd, zh, far = lax.rem(z, 2), lax.div(z, 2), 1 - h
    in_span = BLOCK * (2 * s + c)
    block = 4 * lax.rem(t + z, 2) + 2 * s + c
    across = 4 * (1 - t) + 2 * s + c
    feeder = 6 * (1 - t) + c

    def line(half, dz):
        return half * 32 + x * 8 + lax.rem(z + dz, NZ)

    ys = [(ctx, 2 * lax.rem(y + d, NY) + c) for d in range(1, NY)]
    zs = [(line(h, dz), dp) for dz in range(1, NZ)]
    xs = [(h * 32 + lax.rem(x + d, NX) * 8 + z, dp) for d in range(1, NX)]
    sibling = (ctx, 2 * y + 1 - c)

    def chip(mask):
        t_to = 1 - t if mask & 2 else t
        return 2 * t_to + (1 - s if mask & 1 else s)

    sent = []

    def remote(src, dst, n, to, m=None):
        return pltpu.make_async_remote_copy(
            src_ref=src, dst_ref=dst, send_sem=send.at[n], recv_sem=recv.at[n if m is None else m],
            device_id=to, device_id_type=MESH,
        )

    def go(copy):
        copy.start()
        sent.append(copy)
        return copy

    rows = pl.ds(pl.multiple_of(block * BLOCK, BLOCK), BLOCK)
    mine = kv.at[h, x, odd, zh]
    local_kv = [
        pltpu.make_async_copy(k_hbm.at[rows, :], mine.at[:, 0:HD], loc.at[0]),
        pltpu.make_async_copy(v_hbm.at[rows, :], mine.at[:, HD : 2 * HD], loc.at[1]),
    ]
    local_qg = [
        pltpu.make_async_copy(
            ref.at[span * SPAN : (span + 1) * SPAN, head * HD : (head + 1) * HD],
            qg.at[dp, kind, span, head * SPAN : (head + 1) * SPAN, :],
            loc.at[2 + 4 * kind + 2 * span + head],
        )
        for kind, ref in enumerate((q_hbm, g_hbm))
        for span in range(2)
        for head in range(2)
    ]
    local_lens = pltpu.make_async_copy(lens_hbm, lens, loc.at[10])

    barrier = pltpu.get_barrier_semaphore()
    source = jnp.where(odd == 1, across, dp)
    partners = [*zs, *xs, *ys, sibling]
    others = [(line(far, 0), feeder), (line(far, 0), source)]
    for to in partners + others:
        pl.semaphore_signal(barrier, inc=1, device_id=to, device_id_type=MESH)

    @pl.when(odd == 1)
    def _():
        for to, _ in zs:
            pl.semaphore_signal(barrier, inc=1, device_id=(to, across), device_id_type=MESH)

    for copy in local_kv + local_qg + [local_lens]:
        copy.start()
    pl.semaphore_wait(barrier, len(partners) + 5 - odd + jnp.where(s == t, 2, 0))

    feed = []
    for to_s in range(2):
        of = 4 * lax.rem(1 - t + z, 2) + 2 * to_s + c
        of_rows = pl.ds(pl.multiple_of(of * BLOCK, BLOCK), BLOCK)
        to = (line(far, 0), 4 * (1 - t) + 2 * to_s + c)
        for kind, ref in enumerate((k_hbm, v_hbm)):
            half = mine.at[:, kind * HD : (kind + 1) * HD]
            feed.append(remote(ref.at[of_rows, :], half, 2 * to_s + kind, to, kind))

    for copy in local_qg:
        copy.wait()
    own = qg.at[dp]
    to_y = {mask: go(remote(own, own, 11 + mask, (ctx, 2 * chip(mask) + c))) for mask in (2, 3, 1)}

    @pl.when(s == t)
    def _():
        for copy in feed:
            copy.start()

    for copy in local_kv:
        copy.wait()
    to_z = [go(remote(mine, mine, 3 + dz, zs[dz - 1])) for dz in range(1, NZ)]
    to_sib = {0: go(remote(own, own, 11, sibling))}
    theirs = kv.at[far, x, odd, zh]
    for copy in feed[0:2]:
        copy.wait_recv()
    to_zf = [go(remote(theirs, theirs, 14 + dz, zs[dz - 1])) for dz in range(1, NZ)]
    for copy in to_z:
        copy.wait_recv()
    plane = kv.at[h, x]
    to_x = [go(remote(plane, plane, 21 + d, xs[d - 1])) for d in range(1, NX)]
    for copy in to_zf:
        copy.wait_recv()
    plane_f = kv.at[far, x]
    to_xf = [go(remote(plane_f, plane_f, 24 + d, xs[d - 1])) for d in range(1, NX)]

    local_lens.wait()
    token = lax.rem(lax.broadcasted_iota(jnp.int32, (1, ROWS), 1), SPAN)
    for span, first in ((0, ctx * SPAN), (1, (LAST - ctx) * SPAN)):
        pos = first + token
        begin = jnp.zeros_like(pos)
        end = jnp.int32(0)
        for n in range(NDOCS):
            end = end + lens[n]
            begin = jnp.where(pos >= end, end, begin)
        qpos[span] = pos
        qbeg[span] = begin
    run[0] = jnp.full(run.shape[1:], FLOOR, F32)
    run[1] = jnp.zeros(run.shape[1:], F32)
    run[2] = jnp.zeros(run.shape[1:], F32)

    n_tiles = jnp.where((h == 1) | (ctx >= LAST - REACH - 31), 5, 4)
    row = lax.broadcasted_iota(jnp.int32, (TILE, 1), 0)
    row_ctx = 8 * lax.div(row, 64) + 2 * lax.rem(lax.div(row, BLOCK), 4)
    row_in = in_span + lax.rem(row, BLOCK)

    def tile(n, group, per):
        span = jnp.where(n == 0, 1 - h, jnp.where(n == 2, 0, 1))
        half = jnp.where(n == 1, 1 - h, jnp.where(n == 3, 1, 0))
        hi = jnp.where(n < 2, far, h)
        zp = lax.rem(t + half, 2)
        lanes = pl.ds(pl.multiple_of(group * per * PAIR, PAIR), per * PAIR)
        k = kv[hi, :, zp, :, :, 0:HD].reshape(TILE, HD)
        q = qg[pl.ds(per * group, per), 0, span].reshape(per * PAIR, HD)
        g = qg[pl.ds(per * group, per), 1, span].reshape(per * PAIR, HD)
        return span, half, lanes, hi, zp, k, q, g

    def scores(span, half, hi, zp, k, q, g, per):
        v = kv[hi, :, zp, :, :, HD : 2 * HD].reshape(TILE, HD)
        of = hi * 32 + zp + row_ctx
        kpos = jnp.where(half == 0, of, LAST - of) * SPAN + row_in
        live = (kpos <= qpos[span, :, 0 : per * PAIR]) & (kpos >= qbeg[span, :, 0 : per * PAIR])
        logits = dot(k, q, ((1,), (1,))) * (SCALE * LOG2E)
        dweights = dot(v, g, ((1,), (1,)))
        return live, logits, dweights

    def forward(group, first, last):
        def step(n, _):
            span, half, lanes, hi, zp, k, q, g = tile(n, group, PER)
            live, logits, dweights = scores(span, half, hi, zp, k, q, g, PER)
            logits = jnp.where(live, logits, LOW)
            old = run[0, span, :, lanes]
            top = jnp.maximum(old, jnp.max(logits, axis=0, keepdims=True))
            terms = jnp.exp2(logits - top)
            keep = jnp.exp2(old - top)
            kept[0, n, :, lanes] = terms
            kept[1, n, :, lanes] = dweights
            tops[n, :, lanes] = top
            run[0, span, :, lanes] = top
            run[1, span, :, lanes] = run[1, span, :, lanes] * keep + jnp.sum(terms, axis=0, keepdims=True)
            run[2, span, :, lanes] = run[2, span, :, lanes] * keep + jnp.sum(terms * dweights, axis=0, keepdims=True)
            return 0

        lax.fori_loop(first, last, step, 0)

    def pass_on(mask):
        to_y[mask].wait_recv()
        got = qg.at[2 * chip(mask) + c]
        to_sib[mask] = go(remote(got, got, 27 + mask, sibling))

    to_sib[0].wait_recv()
    pass_on(1)
    for copy in to_x:
        copy.wait_recv()
    to_sib[1].wait_recv()
    forward(t, 2, n_tiles)
    for copy in to_xf:
        copy.wait_recv()
    forward(t, 0, 2)
    pass_on(2)
    pass_on(3)
    to_sib[2].wait_recv()
    to_sib[3].wait_recv()
    forward(1 - t, 0, n_tiles)

    for j in range(NDP):
        for kind in range(3):
            for span in range(2):
                stat[j % 2, kind, j // 2 * 2 + span : j // 2 * 2 + span + 1] = run[kind, span, :, j * PAIR : (j + 1) * PAIR]
    to_stat = go(remote(stat.at[1 - c], stat_r, 31, sibling))
    acc[...] = jnp.zeros_like(acc)
    to_stat.wait_recv()

    def merged(parts):
        top = parts[0][0]
        for part in parts[1:]:
            top = jnp.maximum(top, part[0])
        total, moment = jnp.zeros_like(top), jnp.zeros_like(top)
        for part in parts:
            share = jnp.exp2(part[0] - top)
            total = total + share * part[1]
            moment = moment + share * part[2]
        return top, total, moment

    comb[y, 0], comb[y, 1], comb[y, 2] = merged([stat[c], stat_r[...]])
    to_comb = [go(remote(comb.at[y], comb.at[y], 31 + d, ys[d - 1])) for d in range(1, NY)]
    dqa[...] = jnp.zeros_like(dqa)
    for copy in to_comb:
        copy.wait_recv()
    top, total, moment = merged([comb[n] for n in range(NY)])
    fin[c, 0] = top + jnp.log(total) * LOG2E
    fin[c, 1] = moment / total
    to_fin = go(remote(fin.at[c], fin.at[c], 35, sibling))
    to_fin.wait_recv()
    for j in range(NDP):
        for span in range(2):
            lse[span, :, j * PAIR : (j + 1) * PAIR] = fin[j % 2, 0, j // 2 * 2 + span : j // 2 * 2 + span + 1]
            delta[span, :, j * PAIR : (j + 1) * PAIR] = fin[j % 2, 1, j // 2 * 2 + span : j // 2 * 2 + span + 1]

    def backward(n, group, per=PER):
        span, _, lanes, hi, zp, k, q, g = tile(n, group, per)
        weights = kept[0, n, :, lanes] * jnp.exp2(tops[n, :, lanes] - lse[span, :, lanes])
        dlogits = (weights * (kept[1, n, :, lanes] - delta[span, :, lanes])).astype(BF16)
        acc[hi, :, zp, :, :, 0:HD] += dot(dlogits, q, ((1,), (0,))).reshape(NX, 4, BLOCK, HD)
        acc[hi, :, zp, :, :, HD : 2 * HD] += dot(weights.astype(BF16), g, ((1,), (0,))).reshape(NX, 4, BLOCK, HD)
        dqa[span, :, lanes] += dot(k, dlogits, ((0,), (0,)))
        return group

    def over_x(half, at, first):
        copies = []
        for d in range(1, NX):
            x_s[at, d - 1] = acc[half, lax.rem(x + d, NX)].astype(BF16)
            copies.append(go(remote(x_s.at[at, d - 1], x_r.at[at, d - 1], first + d, xs[d - 1])))
        return copies

    def far_tiles(i, _):
        backward(i, 0, NDP)
        return 0

    lax.fori_loop(0, 2, far_tiles, 0)
    to_rxf = over_x(far, 1, 35)

    def heads(j):
        return pl.ds(pl.multiple_of(j * PAIR, PAIR), PAIR)

    def to_core(mask):
        dq_sib[mask] = dqa[:, :, heads(2 * chip(mask) + 1 - c)].astype(BF16)
        return go(remote(dq_sib.at[mask], dq_sib_r.at[mask], 39 + mask, sibling))

    def from_core(mask, copy):
        copy.wait_recv()
        return dqa[:, :, heads(2 * chip(mask) + c)] + dq_sib_r[mask].astype(F32)

    def over_chips(mask, copy):
        dq_s[mask - 1] = from_core(mask, copy).astype(BF16)
        return go(remote(dq_s.at[mask - 1], dq_r.at[mask - 1], 45 + mask, (ctx, 2 * chip(mask) + c)))

    def own_tiles(i, _):
        backward(i, 0, NDP)
        return 0

    lax.fori_loop(2, n_tiles, own_tiles, 0)
    to_ds = {mask: to_core(mask) for mask in (3, 2)}
    to_rx = over_x(h, 0, 42)
    to_dq = [over_chips(mask, to_ds[mask]) for mask in (3, 2)]
    to_ds.update({mask: to_core(mask) for mask in (1, 0)})
    def over_z(half, at, copies):
        for copy in copies:
            copy.wait_recv()
        own_x[at] = acc[half, x] + x_r[at, 0].astype(F32) + x_r[at, 1].astype(F32) + x_r[at, 2].astype(F32)
        return [go(send_z(at, dz)) for dz in range(1, NZ)]

    def send_z(at, dz):
        zz = lax.rem(z + dz, NZ)
        n = NZ * at + dz
        z_s[n] = own_x[at, lax.rem(zz, 2), lax.div(zz, 2)].astype(BF16)
        to = dp if at else jnp.where(lax.rem(zz, 2) == 1, across, dp)
        return remote(z_s.at[n], z_r.at[n], 49 + n, (line(h, dz), to))

    to_rzf = over_z(far, 1, to_rxf)
    to_dq.append(over_chips(1, to_ds[1]))
    dq_own[...] = from_core(0, to_ds[0])

    to_rz = over_z(h, 0, to_rx)
    for copy in to_rzf:
        copy.wait_recv()
    total_far = own_x[1, odd, zh]
    for n in range(NZ + 1, 2 * NZ):
        total_far = total_far + z_r[n].astype(F32)
    z_s[NZ] = total_far.astype(BF16)
    to_rz.append(go(remote(z_s.at[NZ], z_r.at[NZ], 49 + NZ, (line(far, 0), source))))
    z_s[0] = own_x[0, odd, zh].astype(BF16)
    near = remote(z_s.at[0], z_r.at[0], 49, (ctx, across))

    @pl.when(odd == 1)
    def _():
        near.start()

    @pl.when(odd == 0)
    def _():
        z_r[0] = z_s[0]

    for copy in to_dq:
        copy.wait_recv()
    total_dq = SCALE * (dq_own[...] + dq_r[0].astype(F32) + dq_r[1].astype(F32) + dq_r[2].astype(F32))
    for span in range(2):
        tall = total_dq[span].T.astype(BF16)
        for head in range(2):
            dq_out[span * SPAN : (span + 1) * SPAN, head * HD : (head + 1) * HD] = tall[head * SPAN : (head + 1) * SPAN]

    for copy in to_rz:
        copy.wait_recv()

    @pl.when(odd == 1)
    def _():
        near.wait_recv()
        near.wait_send()

    total_kv = z_r[0].astype(F32)
    for n in range(1, NZ + 1):
        total_kv = total_kv + z_r[n].astype(F32)
    dk_out[...] = (SCALE * total_kv[:, 0:HD]).astype(BF16)
    dv_out[...] = total_kv[:, HD : 2 * HD].astype(BF16)

    @pl.when(s == t)
    def _():
        for copy in feed:
            copy.wait_send()

    for copy in sent:
        copy.wait_send()


def hand_on(dq, dk, dv, dq_out, dk_out, dv_out, sem):
    copies = [
        pltpu.make_async_copy(src, dst, sem.at[n])
        for n, (src, dst) in enumerate(((dq, dq_out), (dk, dk_out), (dv, dv_out)))
    ]
    for copy in copies:
        copy.start()
    for copy in copies:
        copy.wait()


def body(queries, keys, values, out_grads, doc_lengths):
    vmem, hbm = pltpu.VMEM, pl.BlockSpec(memory_space=pltpu.HBM)
    whole = pl.BlockSpec(memory_space=pltpu.VMEM)
    shapes = (
        jax.ShapeDtypeStruct(queries.shape, BF16),
        jax.ShapeDtypeStruct((BLOCK, HD), BF16),
        jax.ShapeDtypeStruct((BLOCK, HD), BF16),
    )
    ins = [
        pltpu.with_memory_space_constraint(a, pltpu.HBM)
        for a in (queries, keys, values, out_grads, doc_lengths)
    ]
    made = pl.pallas_call(
        kernel,
        out_shape=shapes,
        in_specs=[hbm] * 5,
        out_specs=(whole, whole, whole),
        scratch_shapes=[
            vmem((NDP, 2, 2, PAIR, HD), BF16),
            vmem((NH, NX, 2, 4, BLOCK, 2 * HD), BF16),
            vmem((NH, NX, 2, 4, BLOCK, 2 * HD), F32),
            vmem((2, HD, ROWS), F32),
            vmem((2, 1, ROWS), jnp.int32),
            vmem((2, 1, ROWS), jnp.int32),
            vmem((2, 5, TILE, ROWS), F32),
            vmem((5, 1, ROWS), F32),
            vmem((3, 2, 1, ROWS), F32),
            vmem((2, 3, 8, PAIR), F32),
            vmem((3, 8, PAIR), F32),
            vmem((NY, 3, 8, PAIR), F32),
            vmem((2, 2, 8, PAIR), F32),
            vmem((2, 1, ROWS), F32),
            vmem((2, 1, ROWS), F32),
            vmem((NY, 2, PAIR, HD), BF16),
            vmem((NY, 2, PAIR, HD), BF16),
            vmem((2, PAIR, HD), F32),
            vmem((NY - 1, 2, PAIR, HD), BF16),
            vmem((NY - 1, 2, PAIR, HD), BF16),
            vmem((2, NX - 1, 2, 4, BLOCK, 2 * HD), BF16),
            vmem((2, NX - 1, 2, 4, BLOCK, 2 * HD), BF16),
            vmem((2, 2, 4, BLOCK, 2 * HD), F32),
            vmem((16, BLOCK, 2 * HD), BF16),
            vmem((16, BLOCK, 2 * HD), BF16),
            pltpu.SMEM((NDOCS,), jnp.int32),
            pltpu.SemaphoreType.DMA((11,)),
            pltpu.SemaphoreType.DMA((65,)),
            pltpu.SemaphoreType.DMA((65,)),
        ],
        compiler_params=pltpu.CompilerParams(
            collective_id=0, has_side_effects=True, vmem_limit_bytes=40 << 20
        ),
    )(*ins)
    return pl.pallas_call(
        hand_on,
        out_shape=shapes,
        in_specs=[whole] * 3,
        out_specs=(hbm, hbm, hbm),
        scratch_shapes=[pltpu.SemaphoreType.DMA((3,))],
        compiler_params=pltpu.CompilerParams(vmem_limit_bytes=16 << 20),
    )(*made)


def solution(mesh):
    return jax.shard_map(
        body,
        mesh=mesh,
        in_specs=(P("ctx", "dp"), P("ctx", None), P("ctx", None), P("ctx", "dp"), P()),
        out_specs=(P("ctx", "dp"), P(("ctx", "dp"), None), P(("ctx", "dp"), None)),
        check_vma=False,
    )
```

```python
import jax
import jax.numpy as jnp
from jax import lax
from jax.experimental import pallas as pl
from jax.experimental.pallas import tpu as pltpu
from jax.sharding import PartitionSpec as P

MESH = pl.DeviceIdType.MESH
NH, NX, NZ, NY = 2, 4, 8, 4
NDP = 2 * NY
HD, SPAN, NDOCS = 128, 64, 32
BLOCK = 16
PAIR = 2 * SPAN
ROWS = NDP * PAIR
PER = 4
TILE = 256
LAST = 127
REACH = 66
LOW, FLOOR = -1e30, -1e29
SCALE = HD**-0.5
LOG2E = 1.4426950408889634
F32, BF16 = jnp.float32, jnp.bfloat16


def dot(a, b, dims):
    return lax.dot_general(a, b, (dims, ((), ())), preferred_element_type=F32)


def kernel(
    q_hbm, k_hbm, v_hbm, g_hbm, lens_hbm,
    dq_out, dk_out, dv_out,
    qg, kv, acc, dqa, qpos, qbeg, kept, tops, run, stat, stat_r, comb, fin, lse, delta,
    dq_sib, dq_sib_r, dq_own, dq_s, dq_r, x_s, x_r, own_x, z_s, z_r,
    lens, loc, send, recv,
):
    ctx, dp = lax.axis_index("ctx"), lax.axis_index("dp")
    h, x, z = lax.div(ctx, 32), lax.rem(lax.div(ctx, 8), 4), lax.rem(ctx, 8)
    y, c = lax.div(dp, 2), lax.rem(dp, 2)
    t, s = lax.div(y, 2), lax.rem(y, 2)
    odd, zh, far = lax.rem(z, 2), lax.div(z, 2), 1 - h
    in_span = BLOCK * (2 * s + c)
    block = 4 * lax.rem(t + z, 2) + 2 * s + c
    across = 4 * (1 - t) + 2 * s + c
    feeder = 6 * (1 - t) + c

    def line(half, dz):
        return half * 32 + x * 8 + lax.rem(z + dz, NZ)

    ys = [(ctx, 2 * lax.rem(y + d, NY) + c) for d in range(1, NY)]
    zs = [(line(h, dz), dp) for dz in range(1, NZ)]
    xs = [(h * 32 + lax.rem(x + d, NX) * 8 + z, dp) for d in range(1, NX)]
    sibling = (ctx, 2 * y + 1 - c)

    def chip(mask):
        t_to = 1 - t if mask & 2 else t
        return 2 * t_to + (1 - s if mask & 1 else s)

    sent = []

    def remote(src, dst, n, to, m=None):
        return pltpu.make_async_remote_copy(
            src_ref=src, dst_ref=dst, send_sem=send.at[n], recv_sem=recv.at[n if m is None else m],
            device_id=to, device_id_type=MESH,
        )

    def go(copy):
        copy.start()
        sent.append(copy)
        return copy

    rows = pl.ds(pl.multiple_of(block * BLOCK, BLOCK), BLOCK)
    mine = kv.at[h, x, odd, zh]
    local_kv = [
        pltpu.make_async_copy(k_hbm.at[rows, :], mine.at[:, 0:HD], loc.at[0]),
        pltpu.make_async_copy(v_hbm.at[rows, :], mine.at[:, HD : 2 * HD], loc.at[1]),
    ]
    local_qg = [
        pltpu.make_async_copy(
            ref.at[span * SPAN : (span + 1) * SPAN, head * HD : (head + 1) * HD],
            qg.at[dp, kind, span, head * SPAN : (head + 1) * SPAN, :],
            loc.at[2 + 4 * kind + 2 * span + head],
        )
        for kind, ref in enumerate((q_hbm, g_hbm))
        for span in range(2)
        for head in range(2)
    ]
    local_lens = pltpu.make_async_copy(lens_hbm, lens, loc.at[10])

    barrier = pltpu.get_barrier_semaphore()
    source = jnp.where(odd == 1, across, dp)
    partners = [*zs, *xs, *ys, sibling]
    others = [(line(far, 0), feeder), (line(far, 0), source)]
    for to in partners + others:
        pl.semaphore_signal(barrier, inc=1, device_id=to, device_id_type=MESH)

    @pl.when(odd == 1)
    def _():
        for to, _ in zs:
            pl.semaphore_signal(barrier, inc=1, device_id=(to, across), device_id_type=MESH)

    for copy in local_kv + local_qg + [local_lens]:
        copy.start()
    pl.semaphore_wait(barrier, len(partners) + 5 - odd + jnp.where(s == t, 2, 0))

    feed = []
    for to_s in range(2):
        of = 4 * lax.rem(1 - t + z, 2) + 2 * to_s + c
        of_rows = pl.ds(pl.multiple_of(of * BLOCK, BLOCK), BLOCK)
        to = (line(far, 0), 4 * (1 - t) + 2 * to_s + c)
        for kind, ref in enumerate((k_hbm, v_hbm)):
            half = mine.at[:, kind * HD : (kind + 1) * HD]
            feed.append(remote(ref.at[of_rows, :], half, 2 * to_s + kind, to, kind))

    for copy in local_qg:
        copy.wait()
    own = qg.at[dp]
    to_y = {}

    def to_chip(mask):
        to_y[mask] = go(remote(own, own, 11 + mask, (ctx, 2 * chip(mask) + c)))

    to_chip(2)
    to_chip(1)

    @pl.when(s == t)
    def _():
        for copy in feed:
            copy.start()

    for copy in local_kv:
        copy.wait()
    to_z = [go(remote(mine, mine, 3 + dz, zs[dz - 1])) for dz in range(1, NZ)]
    to_sib = {0: go(remote(own, own, 11, sibling))}
    theirs = kv.at[far, x, odd, zh]
    for copy in feed[0:2]:
        copy.wait_recv()
    to_zf = [go(remote(theirs, theirs, 14 + dz, zs[dz - 1])) for dz in range(1, NZ)]
    to_chip(3)
    for copy in to_z:
        copy.wait_recv()
    plane = kv.at[h, x]
    to_x = [go(remote(plane, plane, 21 + d, xs[d - 1])) for d in range(1, NX)]
    for copy in to_zf:
        copy.wait_recv()
    plane_f = kv.at[far, x]
    to_xf = [go(remote(plane_f, plane_f, 24 + d, xs[d - 1])) for d in range(1, NX)]

    local_lens.wait()
    token = lax.rem(lax.broadcasted_iota(jnp.int32, (1, ROWS), 1), SPAN)
    for span, first in ((0, ctx * SPAN), (1, (LAST - ctx) * SPAN)):
        pos = first + token
        begin = jnp.zeros_like(pos)
        end = jnp.int32(0)
        for n in range(NDOCS):
            end = end + lens[n]
            begin = jnp.where(pos >= end, end, begin)
        qpos[span] = pos
        qbeg[span] = begin
    run[0] = jnp.full(run.shape[1:], FLOOR, F32)
    run[1] = jnp.zeros(run.shape[1:], F32)
    run[2] = jnp.zeros(run.shape[1:], F32)

    n_tiles = jnp.where((h == 1) | (ctx >= LAST - REACH - 31), 5, 4)
    row = lax.broadcasted_iota(jnp.int32, (TILE, 1), 0)
    row_ctx = 8 * lax.div(row, 64) + 2 * lax.rem(lax.div(row, BLOCK), 4)
    row_in = in_span + lax.rem(row, BLOCK)

    def tile(n, group, per):
        span = jnp.where(n == 0, 1 - h, jnp.where(n == 2, 0, 1))
        half = jnp.where(n == 1, 1 - h, jnp.where(n == 3, 1, 0))
        hi = jnp.where(n < 2, far, h)
        zp = lax.rem(t + half, 2)
        lanes = pl.ds(pl.multiple_of(group * per * PAIR, PAIR), per * PAIR)
        k = kv[hi, :, zp, :, :, 0:HD].reshape(TILE, HD)
        q = qg[pl.ds(per * group, per), 0, span].reshape(per * PAIR, HD)
        g = qg[pl.ds(per * group, per), 1, span].reshape(per * PAIR, HD)
        return span, half, lanes, hi, zp, k, q, g

    def scores(span, half, hi, zp, k, q, g, per):
        v = kv[hi, :, zp, :, :, HD : 2 * HD].reshape(TILE, HD)
        of = hi * 32 + zp + row_ctx
        kpos = jnp.where(half == 0, of, LAST - of) * SPAN + row_in
        live = (kpos <= qpos[span, :, 0 : per * PAIR]) & (kpos >= qbeg[span, :, 0 : per * PAIR])
        logits = dot(k, q, ((1,), (1,))) * (SCALE * LOG2E)
        dweights = dot(v, g, ((1,), (1,)))
        return live, logits, dweights

    def forward(group, first, last):
        def step(n, _):
            span, half, lanes, hi, zp, k, q, g = tile(n, group, PER)
            live, logits, dweights = scores(span, half, hi, zp, k, q, g, PER)
            logits = jnp.where(live, logits, LOW)
            old = run[0, span, :, lanes]
            top = jnp.maximum(old, jnp.max(logits, axis=0, keepdims=True))
            terms = jnp.exp2(logits - top)
            keep = jnp.exp2(old - top)
            kept[0, n, :, lanes] = terms
            kept[1, n, :, lanes] = dweights
            tops[n, :, lanes] = top
            run[0, span, :, lanes] = top
            run[1, span, :, lanes] = run[1, span, :, lanes] * keep + jnp.sum(terms, axis=0, keepdims=True)
            run[2, span, :, lanes] = run[2, span, :, lanes] * keep + jnp.sum(terms * dweights, axis=0, keepdims=True)
            return 0

        lax.fori_loop(first, last, step, 0, unroll=isinstance(last, int))

    def pass_on(mask):
        to_y[mask].wait_recv()
        got = qg.at[2 * chip(mask) + c]
        to_sib[mask] = go(remote(got, got, 27 + mask, sibling))

    to_sib[0].wait_recv()
    pass_on(1)
    for copy in to_x:
        copy.wait_recv()
    to_sib[1].wait_recv()
    forward(t, 2, n_tiles)
    pass_on(2)
    for copy in to_xf:
        copy.wait_recv()
    forward(t, 0, 2)
    pass_on(3)
    to_sib[2].wait_recv()
    to_sib[3].wait_recv()
    forward(1 - t, 0, 4)
    forward(1 - t, 4, n_tiles)

    for j in range(NDP):
        for kind in range(3):
            for span in range(2):
                stat[j % 2, kind, j // 2 * 2 + span : j // 2 * 2 + span + 1] = run[kind, span, :, j * PAIR : (j + 1) * PAIR]
    to_stat = go(remote(stat.at[1 - c], stat_r, 31, sibling))
    acc[...] = jnp.zeros_like(acc)
    to_stat.wait_recv()

    def merged(parts):
        top = parts[0][0]
        for part in parts[1:]:
            top = jnp.maximum(top, part[0])
        total, moment = jnp.zeros_like(top), jnp.zeros_like(top)
        for part in parts:
            share = jnp.exp2(part[0] - top)
            total = total + share * part[1]
            moment = moment + share * part[2]
        return top, total, moment

    comb[y, 0], comb[y, 1], comb[y, 2] = merged([stat[c], stat_r[...]])
    to_comb = [go(remote(comb.at[y], comb.at[y], 31 + d, ys[d - 1])) for d in range(1, NY)]
    dqa[...] = jnp.zeros_like(dqa)
    for copy in to_comb:
        copy.wait_recv()
    top, total, moment = merged([comb[n] for n in range(NY)])
    fin[c, 0] = top + jnp.log(total) * LOG2E
    fin[c, 1] = moment / total
    to_fin = go(remote(fin.at[c], fin.at[c], 35, sibling))
    to_fin.wait_recv()
    for j in range(NDP):
        for span in range(2):
            lse[span, :, j * PAIR : (j + 1) * PAIR] = fin[j % 2, 0, j // 2 * 2 + span : j // 2 * 2 + span + 1]
            delta[span, :, j * PAIR : (j + 1) * PAIR] = fin[j % 2, 1, j // 2 * 2 + span : j // 2 * 2 + span + 1]

    def backward(n, group, per=PER):
        span, _, lanes, hi, zp, k, q, g = tile(n, group, per)
        weights = kept[0, n, :, lanes] * jnp.exp2(tops[n, :, lanes] - lse[span, :, lanes])
        dlogits = (weights * (kept[1, n, :, lanes] - delta[span, :, lanes])).astype(BF16)
        acc[hi, :, zp, :, :, 0:HD] += dot(dlogits, q, ((1,), (0,))).reshape(NX, 4, BLOCK, HD)
        acc[hi, :, zp, :, :, HD : 2 * HD] += dot(weights.astype(BF16), g, ((1,), (0,))).reshape(NX, 4, BLOCK, HD)
        dqa[span, :, lanes] += dot(k, dlogits, ((0,), (0,)))
        return group

    def over_x(half, at, first):
        copies = []
        for d in range(1, NX):
            x_s[at, d - 1] = acc[half, lax.rem(x + d, NX)].astype(BF16)
            copies.append(go(remote(x_s.at[at, d - 1], x_r.at[at, d - 1], first + d, xs[d - 1])))
        return copies

    def far_tiles(i, _):
        backward(i, 0, NDP)
        return 0

    lax.fori_loop(0, 2, far_tiles, 0, unroll=True)
    to_rxf = over_x(far, 1, 35)

    def heads(j):
        return pl.ds(pl.multiple_of(j * PAIR, PAIR), PAIR)

    def to_core(mask):
        dq_sib[mask] = dqa[:, :, heads(2 * chip(mask) + 1 - c)].astype(BF16)
        return go(remote(dq_sib.at[mask], dq_sib_r.at[mask], 39 + mask, sibling))

    def from_core(mask, copy):
        copy.wait_recv()
        return dqa[:, :, heads(2 * chip(mask) + c)] + dq_sib_r[mask].astype(F32)

    def over_chips(mask, copy):
        dq_s[mask - 1] = from_core(mask, copy).astype(BF16)
        return go(remote(dq_s.at[mask - 1], dq_r.at[mask - 1], 45 + mask, (ctx, 2 * chip(mask) + c)))

    def own_tiles(i, _):
        backward(i, 0, NDP)
        return 0

    lax.fori_loop(2, 4, own_tiles, 0, unroll=True)
    lax.fori_loop(4, n_tiles, own_tiles, 0)
    to_ds = {mask: to_core(mask) for mask in (3, 2)}
    to_rx = over_x(h, 0, 42)
    to_dq = [over_chips(mask, to_ds[mask]) for mask in (3, 2)]
    to_ds.update({mask: to_core(mask) for mask in (1, 0)})
    def over_z(half, at, copies):
        for copy in copies:
            copy.wait_recv()
        own_x[at] = acc[half, x] + x_r[at, 0].astype(F32) + x_r[at, 1].astype(F32) + x_r[at, 2].astype(F32)
        return [go(send_z(at, dz)) for dz in range(1, NZ)]

    def send_z(at, dz):
        zz = lax.rem(z + dz, NZ)
        n = NZ * at + dz
        z_s[n] = own_x[at, lax.rem(zz, 2), lax.div(zz, 2)].astype(BF16)
        to = dp if at else jnp.where(lax.rem(zz, 2) == 1, across, dp)
        return remote(z_s.at[n], z_r.at[n], 49 + n, (line(h, dz), to))

    to_rzf = over_z(far, 1, to_rxf)
    to_dq.append(over_chips(1, to_ds[1]))
    dq_own[...] = from_core(0, to_ds[0])

    to_rz = over_z(h, 0, to_rx)
    for copy in to_rzf:
        copy.wait_recv()
    total_far = own_x[1, odd, zh]
    for n in range(NZ + 1, 2 * NZ):
        total_far = total_far + z_r[n].astype(F32)
    z_s[NZ] = total_far.astype(BF16)
    to_rz.append(go(remote(z_s.at[NZ], z_r.at[NZ], 49 + NZ, (line(far, 0), source))))
    z_s[0] = own_x[0, odd, zh].astype(BF16)
    near = remote(z_s.at[0], z_r.at[0], 49, (ctx, across))

    @pl.when(odd == 1)
    def _():
        near.start()

    @pl.when(odd == 0)
    def _():
        z_r[0] = z_s[0]

    for copy in to_dq:
        copy.wait_recv()
    total_dq = SCALE * (dq_own[...] + dq_r[0].astype(F32) + dq_r[1].astype(F32) + dq_r[2].astype(F32))
    for span in range(2):
        tall = total_dq[span].T.astype(BF16)
        for head in range(2):
            dq_out[span * SPAN : (span + 1) * SPAN, head * HD : (head + 1) * HD] = tall[head * SPAN : (head + 1) * SPAN]

    for copy in to_rz:
        copy.wait_recv()

    @pl.when(odd == 1)
    def _():
        near.wait_recv()
        near.wait_send()

    total_kv = z_r[0].astype(F32)
    for n in range(1, NZ + 1):
        total_kv = total_kv + z_r[n].astype(F32)
    dk_out[...] = (SCALE * total_kv[:, 0:HD]).astype(BF16)
    dv_out[...] = total_kv[:, HD : 2 * HD].astype(BF16)

    @pl.when(s == t)
    def _():
        for copy in feed:
            copy.wait_send()

    for copy in sent:
        copy.wait_send()


def hand_on(dq, dk, dv, dq_out, dk_out, dv_out, sem):
    copies = [
        pltpu.make_async_copy(src, dst, sem.at[n])
        for n, (src, dst) in enumerate(((dq, dq_out), (dk, dk_out), (dv, dv_out)))
    ]
    for copy in copies:
        copy.start()
    for copy in copies:
        copy.wait()


def body(queries, keys, values, out_grads, doc_lengths):
    vmem, hbm = pltpu.VMEM, pl.BlockSpec(memory_space=pltpu.HBM)
    whole = pl.BlockSpec(memory_space=pltpu.VMEM)
    shapes = (
        jax.ShapeDtypeStruct(queries.shape, BF16),
        jax.ShapeDtypeStruct((BLOCK, HD), BF16),
        jax.ShapeDtypeStruct((BLOCK, HD), BF16),
    )
    ins = [
        pltpu.with_memory_space_constraint(a, pltpu.HBM)
        for a in (queries, keys, values, out_grads, doc_lengths)
    ]
    made = pl.pallas_call(
        kernel,
        out_shape=shapes,
        in_specs=[hbm] * 5,
        out_specs=(whole, whole, whole),
        scratch_shapes=[
            vmem((NDP, 2, 2, PAIR, HD), BF16),
            vmem((NH, NX, 2, 4, BLOCK, 2 * HD), BF16),
            vmem((NH, NX, 2, 4, BLOCK, 2 * HD), F32),
            vmem((2, HD, ROWS), F32),
            vmem((2, 1, ROWS), jnp.int32),
            vmem((2, 1, ROWS), jnp.int32),
            vmem((2, 5, TILE, ROWS), F32),
            vmem((5, 1, ROWS), F32),
            vmem((3, 2, 1, ROWS), F32),
            vmem((2, 3, 8, PAIR), F32),
            vmem((3, 8, PAIR), F32),
            vmem((NY, 3, 8, PAIR), F32),
            vmem((2, 2, 8, PAIR), F32),
            vmem((2, 1, ROWS), F32),
            vmem((2, 1, ROWS), F32),
            vmem((NY, 2, PAIR, HD), BF16),
            vmem((NY, 2, PAIR, HD), BF16),
            vmem((2, PAIR, HD), F32),
            vmem((NY - 1, 2, PAIR, HD), BF16),
            vmem((NY - 1, 2, PAIR, HD), BF16),
            vmem((2, NX - 1, 2, 4, BLOCK, 2 * HD), BF16),
            vmem((2, NX - 1, 2, 4, BLOCK, 2 * HD), BF16),
            vmem((2, 2, 4, BLOCK, 2 * HD), F32),
            vmem((16, BLOCK, 2 * HD), BF16),
            vmem((16, BLOCK, 2 * HD), BF16),
            pltpu.SMEM((NDOCS,), jnp.int32),
            pltpu.SemaphoreType.DMA((11,)),
            pltpu.SemaphoreType.DMA((65,)),
            pltpu.SemaphoreType.DMA((65,)),
        ],
        compiler_params=pltpu.CompilerParams(
            collective_id=0, has_side_effects=True, vmem_limit_bytes=40 << 20
        ),
    )(*ins)
    return pl.pallas_call(
        hand_on,
        out_shape=shapes,
        in_specs=[whole] * 3,
        out_specs=(hbm, hbm, hbm),
        scratch_shapes=[pltpu.SemaphoreType.DMA((3,))],
        compiler_params=pltpu.CompilerParams(vmem_limit_bytes=16 << 20),
    )(*made)


def solution(mesh):
    return jax.shard_map(
        body,
        mesh=mesh,
        in_specs=(P("ctx", "dp"), P("ctx", None), P("ctx", None), P("ctx", "dp"), P()),
        out_specs=(P("ctx", "dp"), P(("ctx", "dp"), None), P(("ctx", "dp"), None)),
        check_vma=False,
    )
```

```python
import jax
import jax.numpy as jnp
from jax import lax
from jax.experimental import pallas as pl
from jax.experimental.pallas import tpu as pltpu
from jax.sharding import PartitionSpec as P

MESH = pl.DeviceIdType.MESH
NH, NX, NZ, NY = 2, 4, 8, 4
NDP = 2 * NY
HD, SPAN, NDOCS = 128, 64, 32
BLOCK = 16
PAIR = 2 * SPAN
ROWS = NDP * PAIR
PER = 4
TILE = 256
LAST = 127
REACH = 66
LOW, FLOOR = -1e30, -1e29
SCALE = HD**-0.5
LOG2E = 1.4426950408889634
F32, BF16 = jnp.float32, jnp.bfloat16


def dot(a, b, dims):
    return lax.dot_general(a, b, (dims, ((), ())), preferred_element_type=F32)


def kernel(
    q_hbm, k_hbm, v_hbm, g_hbm, lens_hbm,
    dq_out, dk_out, dv_out,
    qg, kv, acc, dqa, qpos, qbeg, kept, tops, run, stat, stat_r, comb, fin, lse, delta,
    dq_sib, dq_sib_r, dq_own, dq_s, dq_r, x_s, x_r, own_x, z_s, z_r,
    lens, loc, send, recv,
):
    ctx, dp = lax.axis_index("ctx"), lax.axis_index("dp")
    h, x, z = lax.div(ctx, 32), lax.rem(lax.div(ctx, 8), 4), lax.rem(ctx, 8)
    y, c = lax.div(dp, 2), lax.rem(dp, 2)
    t, s = lax.div(y, 2), lax.rem(y, 2)
    odd, zh, far = lax.rem(z, 2), lax.div(z, 2), 1 - h
    in_span = BLOCK * (2 * s + c)
    block = 4 * lax.rem(t + z, 2) + 2 * s + c
    across = 4 * (1 - t) + 2 * s + c
    feeder = 6 * (1 - t) + c

    def line(half, dz):
        return half * 32 + x * 8 + lax.rem(z + dz, NZ)

    ys = [(ctx, 2 * lax.rem(y + d, NY) + c) for d in range(1, NY)]
    zs = [(line(h, dz), dp) for dz in range(1, NZ)]
    xs = [(h * 32 + lax.rem(x + d, NX) * 8 + z, dp) for d in range(1, NX)]
    sibling = (ctx, 2 * y + 1 - c)

    def chip(mask):
        t_to = 1 - t if mask & 2 else t
        return 2 * t_to + (1 - s if mask & 1 else s)

    sent = []

    def remote(src, dst, n, to, m=None):
        return pltpu.make_async_remote_copy(
            src_ref=src, dst_ref=dst, send_sem=send.at[n], recv_sem=recv.at[n if m is None else m],
            device_id=to, device_id_type=MESH,
        )

    def go(copy):
        copy.start()
        sent.append(copy)
        return copy

    rows = pl.ds(pl.multiple_of(block * BLOCK, BLOCK), BLOCK)
    mine = kv.at[h, x, odd, zh]
    local_kv = [
        pltpu.make_async_copy(k_hbm.at[rows, :], mine.at[:, 0:HD], loc.at[0]),
        pltpu.make_async_copy(v_hbm.at[rows, :], mine.at[:, HD : 2 * HD], loc.at[1]),
    ]
    local_qg = [
        pltpu.make_async_copy(
            ref.at[span * SPAN : (span + 1) * SPAN, head * HD : (head + 1) * HD],
            qg.at[dp, kind, span, head * SPAN : (head + 1) * SPAN, :],
            loc.at[2 + 4 * kind + 2 * span + head],
        )
        for kind, ref in enumerate((q_hbm, g_hbm))
        for span in range(2)
        for head in range(2)
    ]
    local_lens = pltpu.make_async_copy(lens_hbm, lens, loc.at[10])

    barrier = pltpu.get_barrier_semaphore()
    source = jnp.where(odd == 1, across, dp)
    partners = [*zs, *xs, *ys, sibling]
    others = [(line(far, 0), feeder), (line(far, 0), source)]
    for to in partners + others:
        pl.semaphore_signal(barrier, inc=1, device_id=to, device_id_type=MESH)

    @pl.when(odd == 1)
    def _():
        for to, _ in zs:
            pl.semaphore_signal(barrier, inc=1, device_id=(to, across), device_id_type=MESH)

    for copy in local_kv + local_qg + [local_lens]:
        copy.start()
    pl.semaphore_wait(barrier, len(partners) + 5 - odd + jnp.where(s == t, 2, 0))

    feed = []
    for to_s in range(2):
        of = 4 * lax.rem(1 - t + z, 2) + 2 * to_s + c
        of_rows = pl.ds(pl.multiple_of(of * BLOCK, BLOCK), BLOCK)
        to = (line(far, 0), 4 * (1 - t) + 2 * to_s + c)
        for kind, ref in enumerate((k_hbm, v_hbm)):
            half = mine.at[:, kind * HD : (kind + 1) * HD]
            feed.append(remote(ref.at[of_rows, :], half, 2 * to_s + kind, to, kind))

    for copy in local_qg:
        copy.wait()
    own = qg.at[dp]
    to_y = {}

    def to_chip(mask):
        to_y[mask] = go(remote(own, own, 11 + mask, (ctx, 2 * chip(mask) + c)))

    to_chip(2)
    to_chip(1)

    @pl.when(s == t)
    def _():
        for copy in feed:
            copy.start()

    for copy in local_kv:
        copy.wait()
    to_z = [go(remote(mine, mine, 3 + dz, zs[dz - 1])) for dz in range(1, NZ)]
    to_sib = {0: go(remote(own, own, 11, sibling))}
    theirs = kv.at[far, x, odd, zh]
    for copy in feed[0:2]:
        copy.wait_recv()
    to_zf = [go(remote(theirs, theirs, 14 + dz, zs[dz - 1])) for dz in range(1, NZ)]
    to_chip(3)
    for copy in to_z:
        copy.wait_recv()
    plane = kv.at[h, x]
    to_x = [go(remote(plane, plane, 21 + d, xs[d - 1])) for d in range(1, NX)]
    for copy in to_zf:
        copy.wait_recv()
    plane_f = kv.at[far, x]
    to_xf = [go(remote(plane_f, plane_f, 24 + d, xs[d - 1])) for d in range(1, NX)]

    local_lens.wait()
    token = lax.rem(lax.broadcasted_iota(jnp.int32, (1, ROWS), 1), SPAN)
    for span, first in ((0, ctx * SPAN), (1, (LAST - ctx) * SPAN)):
        pos = first + token
        begin = jnp.zeros_like(pos)
        end = jnp.int32(0)
        for n in range(NDOCS):
            end = end + lens[n]
            begin = jnp.where(pos >= end, end, begin)
        qpos[span] = pos
        qbeg[span] = begin
    run[0] = jnp.full(run.shape[1:], FLOOR, F32)
    run[1] = jnp.zeros(run.shape[1:], F32)
    run[2] = jnp.zeros(run.shape[1:], F32)

    n_tiles = jnp.where((h == 1) | (ctx >= LAST - REACH - 31), 5, 4)
    row = lax.broadcasted_iota(jnp.int32, (TILE, 1), 0)
    row_ctx = 8 * lax.div(row, 64) + 2 * lax.rem(lax.div(row, BLOCK), 4)
    row_in = in_span + lax.rem(row, BLOCK)

    def tile(n, group, per):
        span = jnp.where(n == 0, 1 - h, jnp.where(n == 2, 0, 1))
        half = jnp.where(n == 1, 1 - h, jnp.where(n == 3, 1, 0))
        hi = jnp.where(n < 2, far, h)
        zp = lax.rem(t + half, 2)
        lanes = pl.ds(pl.multiple_of(group * per * PAIR, PAIR), per * PAIR)
        k = kv[hi, :, zp, :, :, 0:HD].reshape(TILE, HD)
        q = qg[pl.ds(per * group, per), 0, span].reshape(per * PAIR, HD)
        g = qg[pl.ds(per * group, per), 1, span].reshape(per * PAIR, HD)
        return span, half, lanes, hi, zp, k, q, g

    def scores(span, half, hi, zp, k, q, g, per):
        v = kv[hi, :, zp, :, :, HD : 2 * HD].reshape(TILE, HD)
        of = hi * 32 + zp + row_ctx
        kpos = jnp.where(half == 0, of, LAST - of) * SPAN + row_in
        live = (kpos <= qpos[span, :, 0 : per * PAIR]) & (kpos >= qbeg[span, :, 0 : per * PAIR])
        logits = dot(k, q, ((1,), (1,))) * (SCALE * LOG2E)
        dweights = dot(v, g, ((1,), (1,)))
        return live, logits, dweights

    def forward(group, first, last):
        def step(n, _):
            span, half, lanes, hi, zp, k, q, g = tile(n, group, PER)
            live, logits, dweights = scores(span, half, hi, zp, k, q, g, PER)
            logits = jnp.where(live, logits, LOW)
            old = run[0, span, :, lanes]
            top = jnp.maximum(old, jnp.max(logits, axis=0, keepdims=True))
            terms = jnp.exp2(logits - top)
            keep = jnp.exp2(old - top)
            kept[0, n, :, lanes] = terms
            kept[1, n, :, lanes] = dweights
            tops[n, :, lanes] = top
            run[0, span, :, lanes] = top
            run[1, span, :, lanes] = run[1, span, :, lanes] * keep + jnp.sum(terms, axis=0, keepdims=True)
            run[2, span, :, lanes] = run[2, span, :, lanes] * keep + jnp.sum(terms * dweights, axis=0, keepdims=True)
            return 0

        lax.fori_loop(first, last, step, 0, unroll=isinstance(last, int))

    def pass_on(mask):
        to_y[mask].wait_recv()
        got = qg.at[2 * chip(mask) + c]
        to_sib[mask] = go(remote(got, got, 27 + mask, sibling))

    to_sib[0].wait_recv()
    pass_on(1)
    for copy in to_x:
        copy.wait_recv()
    to_sib[1].wait_recv()
    forward(t, 2, n_tiles)
    pass_on(2)
    for copy in to_xf:
        copy.wait_recv()
    forward(t, 0, 2)
    pass_on(3)
    to_sib[2].wait_recv()
    to_sib[3].wait_recv()
    forward(1 - t, 0, 4)
    forward(1 - t, 4, n_tiles)

    for j in range(NDP):
        for kind in range(3):
            for span in range(2):
                stat[j % 2, kind, j // 2 * 2 + span : j // 2 * 2 + span + 1] = run[kind, span, :, j * PAIR : (j + 1) * PAIR]
    to_stat = go(remote(stat.at[1 - c], stat_r, 31, sibling))
    acc[...] = jnp.zeros_like(acc)
    to_stat.wait_recv()

    def merged(parts):
        top = parts[0][0]
        for part in parts[1:]:
            top = jnp.maximum(top, part[0])
        total, moment = jnp.zeros_like(top), jnp.zeros_like(top)
        for part in parts:
            share = jnp.exp2(part[0] - top)
            total = total + share * part[1]
            moment = moment + share * part[2]
        return top, total, moment

    comb[y, 0], comb[y, 1], comb[y, 2] = merged([stat[c], stat_r[...]])
    to_comb = [go(remote(comb.at[y], comb.at[y], 31 + d, ys[d - 1])) for d in range(1, NY)]
    dqa[...] = jnp.zeros_like(dqa)
    for copy in to_comb:
        copy.wait_recv()
    top, total, moment = merged([comb[n] for n in range(NY)])
    fin[c, 0] = top + jnp.log(total) * LOG2E
    fin[c, 1] = moment / total
    to_fin = go(remote(fin.at[c], fin.at[c], 35, sibling))
    to_fin.wait_recv()
    for j in range(NDP):
        for span in range(2):
            lse[span, :, j * PAIR : (j + 1) * PAIR] = fin[j % 2, 0, j // 2 * 2 + span : j // 2 * 2 + span + 1]
            delta[span, :, j * PAIR : (j + 1) * PAIR] = fin[j % 2, 1, j // 2 * 2 + span : j // 2 * 2 + span + 1]

    def backward(n, group, per=PER):
        span, _, lanes, hi, zp, k, q, g = tile(n, group, per)
        weights = kept[0, n, :, lanes] * jnp.exp2(tops[n, :, lanes] - lse[span, :, lanes])
        dlogits = (weights * (kept[1, n, :, lanes] - delta[span, :, lanes])).astype(BF16)
        acc[hi, :, zp, :, :, 0:HD] += dot(dlogits, q, ((1,), (0,))).reshape(NX, 4, BLOCK, HD)
        acc[hi, :, zp, :, :, HD : 2 * HD] += dot(weights.astype(BF16), g, ((1,), (0,))).reshape(NX, 4, BLOCK, HD)
        dqa[span, :, lanes] += dot(k, dlogits, ((0,), (0,)))
        return group

    def over_x(half, at, first):
        copies = []
        for d in range(1, NX):
            x_s[at, d - 1] = acc[half, lax.rem(x + d, NX)].astype(BF16)
            copies.append(go(remote(x_s.at[at, d - 1], x_r.at[at, d - 1], first + d, xs[d - 1])))
        return copies

    def far_tiles(i, _):
        backward(i, 0, NDP)
        return 0

    lax.fori_loop(0, 2, far_tiles, 0, unroll=True)
    to_rxf = over_x(far, 1, 35)

    def heads(j):
        return pl.ds(pl.multiple_of(j * PAIR, PAIR), PAIR)

    def to_core(mask):
        dq_sib[mask] = dqa[:, :, heads(2 * chip(mask) + 1 - c)].astype(BF16)
        return go(remote(dq_sib.at[mask], dq_sib_r.at[mask], 39 + mask, sibling))

    def from_core(mask, copy):
        copy.wait_recv()
        return dqa[:, :, heads(2 * chip(mask) + c)] + dq_sib_r[mask].astype(F32)

    def over_chips(mask, copy):
        dq_s[mask - 1] = from_core(mask, copy).astype(BF16)
        return go(remote(dq_s.at[mask - 1], dq_r.at[mask - 1], 45 + mask, (ctx, 2 * chip(mask) + c)))

    def own_tiles(pair):
        def step(i, _):
            backward(i, pair)
            return 0

        lax.fori_loop(2, 4, step, 0, unroll=True)
        lax.fori_loop(4, n_tiles, step, 0)

    own_tiles(1 - t)
    to_ds = {mask: to_core(mask) for mask in (3, 2)}
    own_tiles(t)
    to_dq = [over_chips(mask, to_ds[mask]) for mask in (3, 2)]
    to_rx = over_x(h, 0, 42)
    to_ds.update({mask: to_core(mask) for mask in (1, 0)})

    def over_z(half, at, copies):
        for copy in copies:
            copy.wait_recv()
        own_x[at] = acc[half, x] + x_r[at, 0].astype(F32) + x_r[at, 1].astype(F32) + x_r[at, 2].astype(F32)
        return [go(send_z(at, dz)) for dz in range(1, NZ)]

    def send_z(at, dz):
        zz = lax.rem(z + dz, NZ)
        n = NZ * at + dz
        z_s[n] = own_x[at, lax.rem(zz, 2), lax.div(zz, 2)].astype(BF16)
        to = dp if at else jnp.where(lax.rem(zz, 2) == 1, across, dp)
        return remote(z_s.at[n], z_r.at[n], 49 + n, (line(h, dz), to))

    to_rzf = over_z(far, 1, to_rxf)
    to_dq.append(over_chips(1, to_ds[1]))
    dq_own[...] = from_core(0, to_ds[0])

    to_rz = over_z(h, 0, to_rx)
    for copy in to_rzf:
        copy.wait_recv()
    total_far = own_x[1, odd, zh]
    for n in range(NZ + 1, 2 * NZ):
        total_far = total_far + z_r[n].astype(F32)
    z_s[NZ] = total_far.astype(BF16)
    to_rz.append(go(remote(z_s.at[NZ], z_r.at[NZ], 49 + NZ, (line(far, 0), source))))
    z_s[0] = own_x[0, odd, zh].astype(BF16)
    near = remote(z_s.at[0], z_r.at[0], 49, (ctx, across))

    @pl.when(odd == 1)
    def _():
        near.start()

    @pl.when(odd == 0)
    def _():
        z_r[0] = z_s[0]

    for copy in to_dq:
        copy.wait_recv()
    total_dq = SCALE * (dq_own[...] + dq_r[0].astype(F32) + dq_r[1].astype(F32) + dq_r[2].astype(F32))
    for span in range(2):
        tall = total_dq[span].T.astype(BF16)
        for head in range(2):
            dq_out[span * SPAN : (span + 1) * SPAN, head * HD : (head + 1) * HD] = tall[head * SPAN : (head + 1) * SPAN]

    for copy in to_rz:
        copy.wait_recv()

    @pl.when(odd == 1)
    def _():
        near.wait_recv()
        near.wait_send()

    total_kv = z_r[0].astype(F32)
    for n in range(1, NZ + 1):
        total_kv = total_kv + z_r[n].astype(F32)
    dk_out[...] = (SCALE * total_kv[:, 0:HD]).astype(BF16)
    dv_out[...] = total_kv[:, HD : 2 * HD].astype(BF16)

    @pl.when(s == t)
    def _():
        for copy in feed:
            copy.wait_send()

    for copy in sent:
        copy.wait_send()


def hand_on(dq, dk, dv, dq_out, dk_out, dv_out, sem):
    copies = [
        pltpu.make_async_copy(src, dst, sem.at[n])
        for n, (src, dst) in enumerate(((dq, dq_out), (dk, dk_out), (dv, dv_out)))
    ]
    for copy in copies:
        copy.start()
    for copy in copies:
        copy.wait()


def body(queries, keys, values, out_grads, doc_lengths):
    vmem, hbm = pltpu.VMEM, pl.BlockSpec(memory_space=pltpu.HBM)
    whole = pl.BlockSpec(memory_space=pltpu.VMEM)
    shapes = (
        jax.ShapeDtypeStruct(queries.shape, BF16),
        jax.ShapeDtypeStruct((BLOCK, HD), BF16),
        jax.ShapeDtypeStruct((BLOCK, HD), BF16),
    )
    ins = [
        pltpu.with_memory_space_constraint(a, pltpu.HBM)
        for a in (queries, keys, values, out_grads, doc_lengths)
    ]
    made = pl.pallas_call(
        kernel,
        out_shape=shapes,
        in_specs=[hbm] * 5,
        out_specs=(whole, whole, whole),
        scratch_shapes=[
            vmem((NDP, 2, 2, PAIR, HD), BF16),
            vmem((NH, NX, 2, 4, BLOCK, 2 * HD), BF16),
            vmem((NH, NX, 2, 4, BLOCK, 2 * HD), F32),
            vmem((2, HD, ROWS), F32),
            vmem((2, 1, ROWS), jnp.int32),
            vmem((2, 1, ROWS), jnp.int32),
            vmem((2, 5, TILE, ROWS), F32),
            vmem((5, 1, ROWS), F32),
            vmem((3, 2, 1, ROWS), F32),
            vmem((2, 3, 8, PAIR), F32),
            vmem((3, 8, PAIR), F32),
            vmem((NY, 3, 8, PAIR), F32),
            vmem((2, 2, 8, PAIR), F32),
            vmem((2, 1, ROWS), F32),
            vmem((2, 1, ROWS), F32),
            vmem((NY, 2, PAIR, HD), BF16),
            vmem((NY, 2, PAIR, HD), BF16),
            vmem((2, PAIR, HD), F32),
            vmem((NY - 1, 2, PAIR, HD), BF16),
            vmem((NY - 1, 2, PAIR, HD), BF16),
            vmem((2, NX - 1, 2, 4, BLOCK, 2 * HD), BF16),
            vmem((2, NX - 1, 2, 4, BLOCK, 2 * HD), BF16),
            vmem((2, 2, 4, BLOCK, 2 * HD), F32),
            vmem((16, BLOCK, 2 * HD), BF16),
            vmem((16, BLOCK, 2 * HD), BF16),
            pltpu.SMEM((NDOCS,), jnp.int32),
            pltpu.SemaphoreType.DMA((11,)),
            pltpu.SemaphoreType.DMA((65,)),
            pltpu.SemaphoreType.DMA((65,)),
        ],
        compiler_params=pltpu.CompilerParams(
            collective_id=0, has_side_effects=True, vmem_limit_bytes=40 << 20
        ),
    )(*ins)
    return pl.pallas_call(
        hand_on,
        out_shape=shapes,
        in_specs=[whole] * 3,
        out_specs=(hbm, hbm, hbm),
        scratch_shapes=[pltpu.SemaphoreType.DMA((3,))],
        compiler_params=pltpu.CompilerParams(vmem_limit_bytes=16 << 20),
    )(*made)


def solution(mesh):
    return jax.shard_map(
        body,
        mesh=mesh,
        in_specs=(P("ctx", "dp"), P("ctx", None), P("ctx", None), P("ctx", "dp"), P()),
        out_specs=(P("ctx", "dp"), P(("ctx", "dp"), None), P(("ctx", "dp"), None)),
        check_vma=False,
    )
```

```python
import jax
import jax.numpy as jnp
from jax import lax
from jax.experimental import pallas as pl
from jax.experimental.pallas import tpu as pltpu
from jax.sharding import PartitionSpec as P

MESH = pl.DeviceIdType.MESH
NH, NX, NZ, NY = 2, 4, 8, 4
NDP = 2 * NY
HD, SPAN, NDOCS = 128, 64, 32
BLOCK = 16
PAIR = 2 * SPAN
ROWS = NDP * PAIR
PER = 4
TILE = 256
LAST = 127
REACH = 66
LOW, FLOOR = -1e30, -1e29
SCALE = HD**-0.5
LOG2E = 1.4426950408889634
F32, BF16 = jnp.float32, jnp.bfloat16


def dot(a, b, dims):
    return lax.dot_general(a, b, (dims, ((), ())), preferred_element_type=F32)


def kernel(
    q_hbm, k_hbm, v_hbm, g_hbm, lens_hbm,
    dq_out, dk_out, dv_out,
    qg, kv, acc, dqa, qpos, qbeg, kept, tops, run, stat, stat_r, comb, fin, lse, delta,
    dq_sib, dq_sib_r, dq_own, dq_s, dq_r, x_s, x_r, own_x, z_s, z_r,
    lens, loc, send, recv,
):
    ctx, dp = lax.axis_index("ctx"), lax.axis_index("dp")
    h, x, z = lax.div(ctx, 32), lax.rem(lax.div(ctx, 8), 4), lax.rem(ctx, 8)
    y, c = lax.div(dp, 2), lax.rem(dp, 2)
    t, s = lax.div(y, 2), lax.rem(y, 2)
    odd, zh, far = lax.rem(z, 2), lax.div(z, 2), 1 - h
    in_span = BLOCK * (2 * s + c)
    block = 4 * lax.rem(t + z, 2) + 2 * s + c
    across = 4 * (1 - t) + 2 * s + c
    feeder = 6 * (1 - t) + c

    def line(half, dz):
        return half * 32 + x * 8 + lax.rem(z + dz, NZ)

    ys = [(ctx, 2 * lax.rem(y + d, NY) + c) for d in range(1, NY)]
    zs = [(line(h, dz), dp) for dz in range(1, NZ)]
    xs = [(h * 32 + lax.rem(x + d, NX) * 8 + z, dp) for d in range(1, NX)]
    sibling = (ctx, 2 * y + 1 - c)

    def chip(mask):
        t_to = 1 - t if mask & 2 else t
        return 2 * t_to + (1 - s if mask & 1 else s)

    sent = []

    def remote(src, dst, n, to, m=None):
        return pltpu.make_async_remote_copy(
            src_ref=src, dst_ref=dst, send_sem=send.at[n], recv_sem=recv.at[n if m is None else m],
            device_id=to, device_id_type=MESH,
        )

    def go(copy):
        copy.start()
        sent.append(copy)
        return copy

    rows = pl.ds(pl.multiple_of(block * BLOCK, BLOCK), BLOCK)
    mine = kv.at[h, x, odd, zh]
    local_kv = [
        pltpu.make_async_copy(k_hbm.at[rows, :], mine.at[:, 0:HD], loc.at[0]),
        pltpu.make_async_copy(v_hbm.at[rows, :], mine.at[:, HD : 2 * HD], loc.at[1]),
    ]
    local_qg = [
        pltpu.make_async_copy(
            ref.at[span * SPAN : (span + 1) * SPAN, head * HD : (head + 1) * HD],
            qg.at[dp, kind, span, head * SPAN : (head + 1) * SPAN, :],
            loc.at[2 + 4 * kind + 2 * span + head],
        )
        for kind, ref in enumerate((q_hbm, g_hbm))
        for span in range(2)
        for head in range(2)
    ]
    local_lens = pltpu.make_async_copy(lens_hbm, lens, loc.at[10])

    barrier = pltpu.get_barrier_semaphore()
    source = jnp.where(odd == 1, across, dp)
    partners = [*zs, *xs, *ys, sibling]
    others = [(line(far, 0), feeder), (line(far, 0), source)]
    for to in partners + others:
        pl.semaphore_signal(barrier, inc=1, device_id=to, device_id_type=MESH)

    @pl.when(odd == 1)
    def _():
        for to, _ in zs:
            pl.semaphore_signal(barrier, inc=1, device_id=(to, across), device_id_type=MESH)

    for copy in local_kv + local_qg + [local_lens]:
        copy.start()
    pl.semaphore_wait(barrier, len(partners) + 5 - odd + jnp.where(s == t, 2, 0))

    feed = []
    for to_s in range(2):
        of = 4 * lax.rem(1 - t + z, 2) + 2 * to_s + c
        of_rows = pl.ds(pl.multiple_of(of * BLOCK, BLOCK), BLOCK)
        to = (line(far, 0), 4 * (1 - t) + 2 * to_s + c)
        for kind, ref in enumerate((k_hbm, v_hbm)):
            half = mine.at[:, kind * HD : (kind + 1) * HD]
            feed.append(remote(ref.at[of_rows, :], half, 2 * to_s + kind, to, kind))

    for copy in local_qg:
        copy.wait()
    own = qg.at[dp]
    to_y = {}

    def to_chip(mask):
        to_y[mask] = go(remote(own, own, 11 + mask, (ctx, 2 * chip(mask) + c)))

    to_chip(2)
    to_chip(1)

    @pl.when(s == t)
    def _():
        for copy in feed:
            copy.start()

    for copy in local_kv:
        copy.wait()
    to_z = [go(remote(mine, mine, 3 + dz, zs[dz - 1])) for dz in range(1, NZ)]
    to_sib = {0: go(remote(own, own, 11, sibling))}
    theirs = kv.at[far, x, odd, zh]
    for copy in feed[0:2]:
        copy.wait_recv()
    to_zf = [go(remote(theirs, theirs, 14 + dz, zs[dz - 1])) for dz in range(1, NZ)]
    to_chip(3)
    for copy in to_z:
        copy.wait_recv()
    plane = kv.at[h, x]
    to_x = [go(remote(plane, plane, 21 + d, xs[d - 1])) for d in range(1, NX)]
    for copy in to_zf:
        copy.wait_recv()
    plane_f = kv.at[far, x]
    to_xf = [go(remote(plane_f, plane_f, 24 + d, xs[d - 1])) for d in range(1, NX)]

    local_lens.wait()
    token = lax.rem(lax.broadcasted_iota(jnp.int32, (1, ROWS), 1), SPAN)
    for span, first in ((0, ctx * SPAN), (1, (LAST - ctx) * SPAN)):
        pos = first + token
        begin = jnp.zeros_like(pos)
        end = jnp.int32(0)
        for n in range(NDOCS):
            end = end + lens[n]
            begin = jnp.where(pos >= end, end, begin)
        qpos[span] = pos
        qbeg[span] = begin
    run[0] = jnp.full(run.shape[1:], FLOOR, F32)
    run[1] = jnp.zeros(run.shape[1:], F32)
    run[2] = jnp.zeros(run.shape[1:], F32)

    n_tiles = jnp.where((h == 1) | (ctx >= LAST - REACH - 31), 5, 4)
    row = lax.broadcasted_iota(jnp.int32, (TILE, 1), 0)
    row_ctx = 8 * lax.div(row, 64) + 2 * lax.rem(lax.div(row, BLOCK), 4)
    row_in = in_span + lax.rem(row, BLOCK)

    def tile(n, group, per):
        span = jnp.where(n == 0, 1 - h, jnp.where(n == 2, 0, 1))
        half = jnp.where(n == 1, 1 - h, jnp.where(n == 3, 1, 0))
        hi = jnp.where(n < 2, far, h)
        zp = lax.rem(t + half, 2)
        lanes = pl.ds(pl.multiple_of(group * per * PAIR, PAIR), per * PAIR)
        k = kv[hi, :, zp, :, :, 0:HD].reshape(TILE, HD)
        q = qg[pl.ds(per * group, per), 0, span].reshape(per * PAIR, HD)
        g = qg[pl.ds(per * group, per), 1, span].reshape(per * PAIR, HD)
        return span, half, lanes, hi, zp, k, q, g

    def scores(span, half, hi, zp, k, q, g, per):
        v = kv[hi, :, zp, :, :, HD : 2 * HD].reshape(TILE, HD)
        of = hi * 32 + zp + row_ctx
        kpos = jnp.where(half == 0, of, LAST - of) * SPAN + row_in
        live = (kpos <= qpos[span, :, 0 : per * PAIR]) & (kpos >= qbeg[span, :, 0 : per * PAIR])
        logits = dot(k, q, ((1,), (1,))) * (SCALE * LOG2E)
        dweights = dot(v, g, ((1,), (1,)))
        return live, logits, dweights

    def forward(group, first, last):
        def step(n, _):
            span, half, lanes, hi, zp, k, q, g = tile(n, group, PER)
            live, logits, dweights = scores(span, half, hi, zp, k, q, g, PER)
            logits = jnp.where(live, logits, LOW)
            old = run[0, span, :, lanes]
            top = jnp.maximum(old, jnp.max(logits, axis=0, keepdims=True))
            terms = jnp.exp2(logits - top)
            keep = jnp.exp2(old - top)
            kept[0, n, :, lanes] = terms
            kept[1, n, :, lanes] = dweights
            tops[n, :, lanes] = top
            run[0, span, :, lanes] = top
            run[1, span, :, lanes] = run[1, span, :, lanes] * keep + jnp.sum(terms, axis=0, keepdims=True)
            run[2, span, :, lanes] = run[2, span, :, lanes] * keep + jnp.sum(terms * dweights, axis=0, keepdims=True)
            return 0

        lax.fori_loop(first, last, step, 0, unroll=isinstance(last, int))

    def pass_on(mask):
        to_y[mask].wait_recv()
        got = qg.at[2 * chip(mask) + c]
        to_sib[mask] = go(remote(got, got, 27 + mask, sibling))

    to_sib[0].wait_recv()
    pass_on(1)
    for copy in to_x:
        copy.wait_recv()
    to_sib[1].wait_recv()
    forward(t, 2, n_tiles)
    pass_on(2)
    for copy in to_xf:
        copy.wait_recv()
    forward(t, 0, 2)
    pass_on(3)
    to_sib[2].wait_recv()
    to_sib[3].wait_recv()
    forward(1 - t, 0, 4)
    forward(1 - t, 4, n_tiles)

    for j in range(NDP):
        for kind in range(3):
            for span in range(2):
                stat[j % 2, kind, j // 2 * 2 + span : j // 2 * 2 + span + 1] = run[kind, span, :, j * PAIR : (j + 1) * PAIR]
    to_stat = go(remote(stat.at[1 - c], stat_r, 31, sibling))
    acc[...] = jnp.zeros_like(acc)
    to_stat.wait_recv()

    def merged(parts):
        top = parts[0][0]
        for part in parts[1:]:
            top = jnp.maximum(top, part[0])
        total, moment = jnp.zeros_like(top), jnp.zeros_like(top)
        for part in parts:
            share = jnp.exp2(part[0] - top)
            total = total + share * part[1]
            moment = moment + share * part[2]
        return top, total, moment

    comb[y, 0], comb[y, 1], comb[y, 2] = merged([stat[c], stat_r[...]])
    to_comb = [go(remote(comb.at[y], comb.at[y], 31 + d, ys[d - 1])) for d in range(1, NY)]
    dqa[...] = jnp.zeros_like(dqa)
    for copy in to_comb:
        copy.wait_recv()
    top, total, moment = merged([comb[n] for n in range(NY)])
    fin[c, 0] = top + jnp.log(total) * LOG2E
    fin[c, 1] = moment / total
    to_fin = go(remote(fin.at[c], fin.at[c], 35, sibling))
    to_fin.wait_recv()
    for j in range(NDP):
        for span in range(2):
            lse[span, :, j * PAIR : (j + 1) * PAIR] = fin[j % 2, 0, j // 2 * 2 + span : j // 2 * 2 + span + 1]
            delta[span, :, j * PAIR : (j + 1) * PAIR] = fin[j % 2, 1, j // 2 * 2 + span : j // 2 * 2 + span + 1]

    def backward(n, group, per=PER):
        span, _, lanes, hi, zp, k, q, g = tile(n, group, per)
        weights = kept[0, n, :, lanes] * jnp.exp2(tops[n, :, lanes] - lse[span, :, lanes])
        dlogits = (weights * (kept[1, n, :, lanes] - delta[span, :, lanes])).astype(BF16)
        acc[hi, :, zp, :, :, 0:HD] += dot(dlogits, q, ((1,), (0,))).reshape(NX, 4, BLOCK, HD)
        acc[hi, :, zp, :, :, HD : 2 * HD] += dot(weights.astype(BF16), g, ((1,), (0,))).reshape(NX, 4, BLOCK, HD)
        dqa[span, :, lanes] += dot(k, dlogits, ((0,), (0,)))
        return group

    def over_x(half, at, first):
        copies = []
        for d in range(1, NX):
            x_s[at, d - 1] = acc[half, lax.rem(x + d, NX)].astype(BF16)
            copies.append(go(remote(x_s.at[at, d - 1], x_r.at[at, d - 1], first + d, xs[d - 1])))
        return copies

    def far_tiles(i, _):
        backward(i, 0, NDP)
        return 0

    lax.fori_loop(0, 2, far_tiles, 0, unroll=True)
    to_rxf = over_x(far, 1, 35)

    def heads(j):
        return pl.ds(pl.multiple_of(j * PAIR, PAIR), PAIR)

    def to_core(mask):
        dq_sib[mask] = dqa[:, :, heads(2 * chip(mask) + 1 - c)].astype(BF16)
        return go(remote(dq_sib.at[mask], dq_sib_r.at[mask], 39 + mask, sibling))

    def from_core(mask, copy):
        copy.wait_recv()
        return dqa[:, :, heads(2 * chip(mask) + c)] + dq_sib_r[mask].astype(F32)

    def over_chips(mask, copy):
        dq_s[mask - 1] = from_core(mask, copy).astype(BF16)
        return go(remote(dq_s.at[mask - 1], dq_r.at[mask - 1], 45 + mask, (ctx, 2 * chip(mask) + c)))

    def own_tiles(pair):
        def step(i, _):
            backward(i, pair)
            return 0

        lax.fori_loop(2, 4, step, 0, unroll=True)
        lax.fori_loop(4, n_tiles, step, 0)

    own_tiles(1 - t)
    to_ds = {mask: to_core(mask) for mask in (3, 2)}
    own_tiles(t)
    to_dq = [over_chips(mask, to_ds[mask]) for mask in (3, 2)]
    to_ds.update({mask: to_core(mask) for mask in (1, 0)})
    to_rx = over_x(h, 0, 42)

    def over_z(half, at, copies):
        for copy in copies:
            copy.wait_recv()
        own_x[at] = acc[half, x] + x_r[at, 0].astype(F32) + x_r[at, 1].astype(F32) + x_r[at, 2].astype(F32)
        return [go(send_z(at, dz)) for dz in range(1, NZ)]

    def send_z(at, dz):
        zz = lax.rem(z + dz, NZ)
        n = NZ * at + dz
        z_s[n] = own_x[at, lax.rem(zz, 2), lax.div(zz, 2)].astype(BF16)
        to = dp if at else jnp.where(lax.rem(zz, 2) == 1, across, dp)
        return remote(z_s.at[n], z_r.at[n], 49 + n, (line(h, dz), to))

    to_rzf = over_z(far, 1, to_rxf)
    to_dq.append(over_chips(1, to_ds[1]))
    dq_own[...] = from_core(0, to_ds[0])

    to_rz = over_z(h, 0, to_rx)
    for copy in to_rzf:
        copy.wait_recv()
    total_far = own_x[1, odd, zh]
    for n in range(NZ + 1, 2 * NZ):
        total_far = total_far + z_r[n].astype(F32)
    z_s[NZ] = total_far.astype(BF16)
    to_rz.append(go(remote(z_s.at[NZ], z_r.at[NZ], 49 + NZ, (line(far, 0), source))))
    z_s[0] = own_x[0, odd, zh].astype(BF16)
    near = remote(z_s.at[0], z_r.at[0], 49, (ctx, across))

    @pl.when(odd == 1)
    def _():
        near.start()

    @pl.when(odd == 0)
    def _():
        z_r[0] = z_s[0]

    for copy in to_dq:
        copy.wait_recv()
    total_dq = SCALE * (dq_own[...] + dq_r[0].astype(F32) + dq_r[1].astype(F32) + dq_r[2].astype(F32))
    for span in range(2):
        tall = total_dq[span].T.astype(BF16)
        for head in range(2):
            dq_out[span * SPAN : (span + 1) * SPAN, head * HD : (head + 1) * HD] = tall[head * SPAN : (head + 1) * SPAN]

    for copy in to_rz:
        copy.wait_recv()

    @pl.when(odd == 1)
    def _():
        near.wait_recv()
        near.wait_send()

    total_kv = z_r[0].astype(F32)
    for n in range(1, NZ + 1):
        total_kv = total_kv + z_r[n].astype(F32)
    dk_out[...] = (SCALE * total_kv[:, 0:HD]).astype(BF16)
    dv_out[...] = total_kv[:, HD : 2 * HD].astype(BF16)

    @pl.when(s == t)
    def _():
        for copy in feed:
            copy.wait_send()

    for copy in sent:
        copy.wait_send()


def hand_on(dq, dk, dv, dq_out, dk_out, dv_out, sem):
    copies = [
        pltpu.make_async_copy(src, dst, sem.at[n])
        for n, (src, dst) in enumerate(((dq, dq_out), (dk, dk_out), (dv, dv_out)))
    ]
    for copy in copies:
        copy.start()
    for copy in copies:
        copy.wait()


def body(queries, keys, values, out_grads, doc_lengths):
    vmem, hbm = pltpu.VMEM, pl.BlockSpec(memory_space=pltpu.HBM)
    whole = pl.BlockSpec(memory_space=pltpu.VMEM)
    shapes = (
        jax.ShapeDtypeStruct(queries.shape, BF16),
        jax.ShapeDtypeStruct((BLOCK, HD), BF16),
        jax.ShapeDtypeStruct((BLOCK, HD), BF16),
    )
    ins = [
        pltpu.with_memory_space_constraint(a, pltpu.HBM)
        for a in (queries, keys, values, out_grads, doc_lengths)
    ]
    made = pl.pallas_call(
        kernel,
        out_shape=shapes,
        in_specs=[hbm] * 5,
        out_specs=(whole, whole, whole),
        scratch_shapes=[
            vmem((NDP, 2, 2, PAIR, HD), BF16),
            vmem((NH, NX, 2, 4, BLOCK, 2 * HD), BF16),
            vmem((NH, NX, 2, 4, BLOCK, 2 * HD), F32),
            vmem((2, HD, ROWS), F32),
            vmem((2, 1, ROWS), jnp.int32),
            vmem((2, 1, ROWS), jnp.int32),
            vmem((2, 5, TILE, ROWS), F32),
            vmem((5, 1, ROWS), F32),
            vmem((3, 2, 1, ROWS), F32),
            vmem((2, 3, 8, PAIR), F32),
            vmem((3, 8, PAIR), F32),
            vmem((NY, 3, 8, PAIR), F32),
            vmem((2, 2, 8, PAIR), F32),
            vmem((2, 1, ROWS), F32),
            vmem((2, 1, ROWS), F32),
            vmem((NY, 2, PAIR, HD), BF16),
            vmem((NY, 2, PAIR, HD), BF16),
            vmem((2, PAIR, HD), F32),
            vmem((NY - 1, 2, PAIR, HD), BF16),
            vmem((NY - 1, 2, PAIR, HD), BF16),
            vmem((2, NX - 1, 2, 4, BLOCK, 2 * HD), BF16),
            vmem((2, NX - 1, 2, 4, BLOCK, 2 * HD), BF16),
            vmem((2, 2, 4, BLOCK, 2 * HD), F32),
            vmem((16, BLOCK, 2 * HD), BF16),
            vmem((16, BLOCK, 2 * HD), BF16),
            pltpu.SMEM((NDOCS,), jnp.int32),
            pltpu.SemaphoreType.DMA((11,)),
            pltpu.SemaphoreType.DMA((65,)),
            pltpu.SemaphoreType.DMA((65,)),
        ],
        compiler_params=pltpu.CompilerParams(
            collective_id=0, has_side_effects=True, vmem_limit_bytes=40 << 20
        ),
    )(*ins)
    return pl.pallas_call(
        hand_on,
        out_shape=shapes,
        in_specs=[whole] * 3,
        out_specs=(hbm, hbm, hbm),
        scratch_shapes=[pltpu.SemaphoreType.DMA((3,))],
        compiler_params=pltpu.CompilerParams(vmem_limit_bytes=16 << 20),
    )(*made)


def solution(mesh):
    return jax.shard_map(
        body,
        mesh=mesh,
        in_specs=(P("ctx", "dp"), P("ctx", None), P("ctx", None), P("ctx", "dp"), P()),
        out_specs=(P("ctx", "dp"), P(("ctx", "dp"), None), P(("ctx", "dp"), None)),
        check_vma=False,
    )
```
